768 devices in a mesh: dom: 192 (over y, z, core), grp: 4 (over x).
Axes of the slice: x: 4, y: 8, z: 12, core: 2. Of those that a mesh axis runs over, the one named last changes fastest.
Arguments:
- positions: float32 [3, 98304], P(None, ('dom', 'grp')), may hold values from 0 to 1
- features: bfloat16 [128, 98304], P(None, ('dom', 'grp')), may hold values from -6 to 6
- neighbour_weight: bfloat16 [128, 128], replicated, may hold values from -0.5 to 0.5
- adjoint: bfloat16 [256, 98304], P(None, ('dom', 'grp')), may hold values from -0.119628906 to 0.119628906
- basis_weight: bfloat16 [8, 128], replicated, may hold values from -2 to 2
- edge_weight: bfloat16 [128, 64], replicated, may hold values from -0.5 to 0.5
- tile_center: int32 [3072], P(('dom', 'grp')), may hold values from 0 to 3
- tile_neighbour: int32 [3072], P(('dom', 'grp')), may hold values from 0 to 11, as said below
- tile_count: int32 [768], P(('dom', 'grp')), may hold values from 2 to 4, as said below
Outputs:
- position_grad: float32 [3, 98304], P(None, ('dom', 'grp'))
The draws below stay inside these ranges and needn't reach their ends.
Inputs may be any that keep to these rules, and one draw needn't show every extreme that they name: `tile_count`: some device has all 4 slots live in every draw. `tile_neighbour`: the first slot of every device with an even index s names a block of the lower domain, that of every odd device a block of the upper domain; other slots are uniform over the three domains.
All inputs are finite; a program needn't handle non-finite values.
Results may differ from the reference program's by a relative error of at most 0.0012.
Values may be sent and summed in bfloat16 or wider, within the bound.
A program may use at most 32 MiB of HBM per device.

```python
import jax
import jax.numpy as jnp
from jax import lax

LAT = 128
CH = 64
NB = 8
BLK = 128
BLK_DEV = 1
TILES_DEV = 4
SHARDS = 768
ATOMS = 98304
GROUP_BLOCKS = 4
TILE_SLOTS = 3072
N_DOM = 192
N_GRP = 4


def draw_tile_count(key, part):
    first_key, second_key = jax.random.split(key)
    counts = jax.random.randint(first_key, (SHARDS,), (TILES_DEV + 1) // 2, TILES_DEV + 1)
    busiest = jax.random.randint(second_key, (), 0, SHARDS)
    return jnp.where(jnp.arange(SHARDS) == busiest, TILES_DEV, counts).astype(jnp.int32)


def draw_tile_neighbour(key, part):
    first_key = jax.random.fold_in(key, 11)
    second_key = jax.random.fold_in(key, 12)
    anywhere = jax.random.randint(first_key, (TILE_SLOTS,), 0, 3 * GROUP_BLOCKS)
    block_pick = jax.random.randint(second_key, (TILE_SLOTS,), 0, GROUP_BLOCKS)
    slots = jnp.arange(TILE_SLOTS, dtype=jnp.int32)
    device = slots // TILES_DEV
    slab_pick = 2 * (device % 2)
    first_slot = slots % TILES_DEV == 0
    return jnp.where(first_slot, slab_pick * GROUP_BLOCKS + block_pick, anywhere).astype(jnp.int32)


def touch_ends(values, key, smallest, high):
    dims = values.shape
    place = [jax.random.randint(jax.random.fold_in(key, axis), (), 0, dims[axis]) for axis in range(len(dims))]
    values = values.at[tuple(place)].set(smallest)
    longest = dims.index(max(dims))
    place[longest] = (place[longest] + 1) % dims[longest]
    return values.at[tuple(place)].set(high)


def block_scale(stream_key, shape, cuts, least, high):
    loudness, own = 1.0, jax.random.fold_in(stream_key, 6)
    for dim, parts in cuts:
        heights = jnp.exp(jax.random.uniform(jax.random.fold_in(own, dim), (parts,), jnp.float32, least / len(cuts), high / len(cuts)))
        loudness = loudness * jnp.repeat(heights, shape[dim] // parts).reshape([-1 if axis == dim else 1 for axis in range(len(shape))])
    return loudness


def gaussian(key, shape, width, reach, cuts=(), held_as=jnp.bfloat16):
    factor_of = block_scale(key, shape, cuts, -0.22, 0.18) if cuts else 1.0
    array = jax.random.normal(key, shape, jnp.float32) * width * factor_of
    return jnp.minimum(jnp.maximum(array, -reach), reach).astype(held_as)


def setup_inputs(seed: int = 0) -> dict:
    arg_keys = jax.random.split(jax.random.key(seed), 10)
    positions = jnp.clip(1.0 * jax.random.uniform(arg_keys[0], (3, ATOMS), jnp.float32) ** block_scale(arg_keys[0], (3, ATOMS), ((1, 768),), -0.2, 0.2), 0.0, 1.0)
    features = gaussian(arg_keys[1], (LAT, ATOMS), 1.0, 6.0, ((1, 768),))
    neighbour_weight = gaussian(arg_keys[2], (LAT, LAT), LAT ** -0.5, 0.5)
    adjoint = gaussian(arg_keys[3], (4 * CH, ATOMS), 0.02, 0.119628906, ((1, 768),))
    basis_weight = gaussian(arg_keys[4], (NB, LAT), NB ** -0.5, 2.0)
    edge_weight = gaussian(arg_keys[5], (LAT, CH), LAT ** -0.5, 0.5)
    tile_center = touch_ends(jax.random.randint(arg_keys[6], (TILE_SLOTS,), 0, GROUP_BLOCKS), jax.random.fold_in(arg_keys[6], 1), 0, GROUP_BLOCKS - 1).astype(jnp.int32)
    tile_neighbour = draw_tile_neighbour(jax.random.fold_in(arg_keys[9], 71), 0)
    tile_count = draw_tile_count(jax.random.fold_in(arg_keys[9], 71), 0)
    return dict(positions=positions, features=features, neighbour_weight=neighbour_weight, adjoint=adjoint, basis_weight=basis_weight, edge_weight=edge_weight, tile_center=tile_center, tile_neighbour=tile_neighbour, tile_count=tile_count)


slab_length = 1.0
cutoff_square = 4.0


def decay_rates(basis_count):
    return 0.3 * 1.5 ** jnp.arange(basis_count, dtype=jnp.float32)


def tile_terms(center_pos, neigh_pos, center_feat, neigh_feat, adj_center, basis_weight, edge_weight, self_pair):
    block_size = center_pos.shape[1]
    latent = center_feat.shape[0]
    channels = edge_weight.shape[1]
    basis_count = basis_weight.shape[0]
    displace = neigh_pos[:, None, :] - center_pos[:, :, None]
    dist_sq = jnp.sum(displace * displace, axis=0)
    identity = jnp.eye(block_size, dtype=jnp.float32)
    keep_mask = 1.0 - self_pair * identity
    inner_part = jnp.maximum(1.0 - dist_sq / cutoff_square, 0.0)
    envelope = inner_part * inner_part * keep_mask
    basis_rates = decay_rates(basis_count)
    basis_vals = jnp.exp(-dist_sq[:, :, None] * basis_rates)
    basis_low = basis_vals.astype(jnp.bfloat16)
    pre_act = jnp.dot(basis_low.reshape(-1, basis_count), basis_weight, preferred_element_type=jnp.float32).reshape(block_size, block_size, latent)
    pre_act = pre_act + center_feat.T.astype(jnp.float32)[:, None, :] + neigh_feat.T.astype(jnp.float32)[None, :, :]
    sigmoid_pre = jax.nn.sigmoid(pre_act)
    hidden = (pre_act * sigmoid_pre).astype(jnp.bfloat16)
    weights = jnp.dot(hidden.reshape(-1, latent), edge_weight, preferred_element_type=jnp.float32).reshape(block_size, block_size, channels)
    harmonics = jnp.concatenate([jnp.ones((1, block_size, block_size), jnp.float32), displace * 0.5], axis=0)
    adj_full = adj_center.astype(jnp.float32).reshape(4, channels, block_size)
    projected = jnp.einsum('mci,mij->ijc', adj_full, harmonics)
    gate_grad = (envelope[:, :, None] * projected).astype(jnp.bfloat16)
    along_chan = jnp.einsum('mci,ijc->mij', adj_full, weights)
    harm_grad = envelope[None] * along_chan
    env_grad = jnp.sum(along_chan * harmonics, axis=0)
    hidden_grad = lax.dot_general(gate_grad.reshape(-1, channels), edge_weight, (((1,), (1,)), ((), ())), preferred_element_type=jnp.float32).reshape(block_size, block_size, latent)
    pre_grad = (hidden_grad * sigmoid_pre * (1.0 + pre_act * (1.0 - sigmoid_pre))).astype(jnp.bfloat16)
    basis_grad = lax.dot_general(pre_grad.reshape(-1, latent), basis_weight, (((1,), (1,)), ((), ())), preferred_element_type=jnp.float32).reshape(block_size, block_size, basis_count)
    sq_grad = jnp.sum(basis_grad * basis_vals * (-basis_rates), axis=2) - env_grad * keep_mask * 2.0 * inner_part / cutoff_square
    disp_grad = 2.0 * sq_grad[None] * displace + 0.5 * harm_grad[1:]
    return -jnp.sum(disp_grad, axis=2), jnp.sum(disp_grad, axis=1)


def reference(positions, features, neighbour_weight, adjoint, basis_weight, edge_weight, tile_center, tile_neighbour, tile_count):
    neigh_all = lax.dot_general(neighbour_weight, features, (((0,), (0,)), ((), ())), preferred_element_type=jnp.float32).astype(jnp.bfloat16)
    group_blocks = BLK_DEV * N_GRP

    def tile_step(grad_total, tile_slot):
        device = tile_slot // TILES_DEV
        domain = device // N_GRP
        live_tile = (tile_slot % TILES_DEV < tile_count[device]).astype(jnp.float32)
        center = tile_center[tile_slot]
        neigh_block = tile_neighbour[tile_slot]
        slab_index = neigh_block // group_blocks - 1
        other_dom = jnp.mod(domain + slab_index, N_DOM)
        center_start = ((domain * group_blocks + center) * BLK).astype(jnp.int32)
        neigh_start = ((other_dom * group_blocks + neigh_block % group_blocks) * BLK).astype(jnp.int32)
        zero_row = jnp.zeros((), jnp.float32)
        lift_vec = jnp.stack([zero_row, zero_row, slab_index.astype(jnp.float32) * slab_length])[:, None]
        center_pos = lax.dynamic_slice_in_dim(positions, center_start, BLK, 1)
        neigh_pos = lax.dynamic_slice_in_dim(positions, neigh_start, BLK, 1) + lift_vec
        center_feat = lax.dynamic_slice_in_dim(features, center_start, BLK, 1)
        neigh_feat = lax.dynamic_slice_in_dim(neigh_all, neigh_start, BLK, 1)
        adj_center = lax.dynamic_slice_in_dim(adjoint, center_start, BLK, 1)
        self_pair = (neigh_block == center + group_blocks).astype(jnp.float32)
        center_grad, neigh_grad = tile_terms(center_pos, neigh_pos, center_feat, neigh_feat, adj_center, basis_weight, edge_weight, self_pair)
        old_center = lax.dynamic_slice_in_dim(grad_total, center_start, BLK, 1)
        grad_total = lax.dynamic_update_slice_in_dim(grad_total, old_center + live_tile * center_grad, center_start, 1)
        old_neigh = lax.dynamic_slice_in_dim(grad_total, neigh_start, BLK, 1)
        grad_total = lax.dynamic_update_slice_in_dim(grad_total, old_neigh + live_tile * neigh_grad, neigh_start, 1)
        return grad_total, None

    start_total = jnp.zeros((3, ATOMS), jnp.float32)
    grad_total, unused = lax.scan(tile_step, start_total, jnp.arange(TILE_SLOTS, dtype=jnp.int32))
    return grad_total
```

```python
import jax
import jax.numpy as jnp
from jax import lax
from jax.experimental import pallas as pl
from jax.experimental.pallas import tpu as pltpu
from jax.sharding import PartitionSpec as P

BF = jnp.bfloat16
F32 = jnp.float32
BLK = 128
GRP = 4
SLOTS = 4
NSLOT = GRP * SLOTS
QTR = BLK // GRP
PAIRS = QTR // 2
U = PAIRS // 2
MESH = pl.DeviceIdType.MESH

RATES = tuple(0.3 * 1.5**b for b in range(8))


def pair_values(h, hg):
    one = jnp.asarray(1.0, BF)
    t = jnp.tanh(h)
    p = one + t
    hid = h * p
    return hid, hg * (p + hid * (one - t))


def body(
    pos_in, feat_in, nw_in, adj_in, bw_in, ew_in, tc_in, tn_in, cnt_in, out_ref,
    featx, posx, meta, meta_sm, at_send, at_all, res_send, res_recv,
    nf, ptr, cposb, bt32, bt, lhs, wred, rhs, bas, al, pr, ds, y_s, s2_s, nacc, cacc,
    hb, xb,
    fx_send, fz_send, f_recv, a_send, a_recv, p_send, p_recv, m_send, m_recv,
    r_send, r_recv, loc_sem,
):
    g = lax.axis_index("grp")
    dm = lax.axis_index("dom")
    n_dom = lax.axis_size("dom")
    up = lax.rem(dm + 1, n_dom)
    dn = lax.rem(dm + n_dom - 1, n_dom)
    xs = [lax.rem(g + j, GRP) for j in range(1, GRP)]
    barrier = pltpu.get_barrier_semaphore()
    for x in xs:
        pl.semaphore_signal(barrier, inc=1, device_id=(dm, x), device_id_type=MESH)
    for d in (up, dn):
        for x in range(GRP):
            pl.semaphore_signal(barrier, inc=1, device_id=(d, x), device_id_type=MESH)

    lane8 = lax.broadcasted_iota(jnp.int32, (8, BLK), 1)
    sub8 = lax.broadcasted_iota(jnp.int32, (8, BLK), 0)
    mv = jnp.zeros((8, BLK), jnp.int32)
    for t in range(SLOTS):
        mv = jnp.where(lane8 == t, tc_in[t], mv)
        mv = jnp.where(lane8 == SLOTS + t, tn_in[t], mv)
    meta[g] = jnp.where(lane8 == 2 * SLOTS, cnt_in[0], mv)
    posx[GRP + g] = jnp.concatenate([pos_in[...], jnp.zeros((5, BLK), F32)], 0)
    at_send[...] = adj_in[...].astype(F32).T.astype(BF)

    pl.semaphore_wait(barrier, 11)

    def rcopy(src, dst, ss, rs, dev):
        return pltpu.make_async_remote_copy(
            src_ref=src, dst_ref=dst, send_sem=ss, recv_sem=rs, device_id=dev, device_id_type=MESH
        )

    sends = []

    def go(c):
        c.start()
        sends.append(c)

    own = GRP + g
    for j, x in enumerate(xs):
        go(rcopy(posx.at[own], posx.at[own], p_send.at[j], p_recv.at[own], (dm, x)))
        go(rcopy(meta.at[g], meta.at[g], m_send.at[j], m_recv.at[g], (dm, x)))
    for x in range(GRP):
        go(rcopy(posx.at[own], posx.at[g], p_send.at[3 + x], p_recv.at[g], (up, x)))
        go(rcopy(posx.at[own], posx.at[2 * GRP + g], p_send.at[7 + x], p_recv.at[2 * GRP + g], (dn, x)))
    for j, x in enumerate(xs):
        rows = pl.ds(pl.multiple_of(QTR * x, QTR), QTR)
        go(rcopy(at_send.at[rows, :], at_all.at[g], a_send.at[j], a_recv.at[g], (dm, x)))
    for j, x in enumerate((xs[0], xs[2], xs[1])):
        go(rcopy(feat_in, featx.at[own], fx_send.at[j], f_recv.at[own], (dm, x)))
    go(rcopy(feat_in, featx.at[g], fz_send.at[0], f_recv.at[g], (up, g)))
    go(rcopy(feat_in, featx.at[2 * GRP + g], fz_send.at[1], f_recv.at[2 * GRP + g], (dn, g)))

    featx[own] = feat_in[...]
    at_all[g] = at_send[pl.ds(pl.multiple_of(QTR * g, QTR), QTR), :]
    wred[...] = jnp.concatenate(
        [
            jnp.concatenate([jnp.zeros((8, BLK), F32), bw_in[...].astype(F32)], 1),
            jnp.zeros((8, 2 * BLK), F32),
        ],
        0,
    ).astype(BF)
    nacc[...] = jnp.zeros_like(nacc)
    cacc[...] = jnp.zeros_like(cacc)

    for x in xs:
        rcopy(at_all.at[x], at_all.at[x], a_send.at[0], a_recv.at[x], (dm, x)).wait_recv()
    at2 = at_all[...].reshape(BLK, 4 * 64)
    for m in range(4):
        bm = lax.dot_general(
            at2[:, 64 * m : 64 * m + 64], ew_in[...], (((1,), (1,)), ((), ())), preferred_element_type=F32
        )
        hi = bm.astype(BF).astype(F32)
        bt32[pl.ds(m, BLK, stride=8), :] = hi
        bt32[pl.ds(4 + m, BLK, stride=8), :] = bm - hi

    for j, x in enumerate((xs[0], xs[2], xs[1])):
        blk = GRP + x
        rcopy(featx.at[blk], featx.at[blk], fx_send.at[0], f_recv.at[blk], (dm, x)).wait_recv()
        go(rcopy(featx.at[blk], featx.at[x], fz_send.at[2 + 2 * j], f_recv.at[x], (up, g)))
        go(rcopy(featx.at[blk], featx.at[2 * GRP + x], fz_send.at[3 + 2 * j], f_recv.at[2 * GRP + x], (dn, g)))

    lane = lax.broadcasted_iota(jnp.int32, (BLK, BLK), 1)
    wt = (
        jnp.concatenate([bw_in[...].astype(F32), jnp.zeros((BLK - 8, BLK), F32)], 0).T * 0.5
    )
    for c in range(GRP):
        fr = pltpu.roll(featx[GRP + c].astype(F32) * 0.5, lax.rem(8 + BLK - QTR * g, BLK), 1)
        for w in range(2):
            wr = bt32[1024 // 8 * (2 * c + w) : 1024 // 8 * (2 * c + w + 1), :].T
            for r in range(8):
                cp = 16 * c + 8 * w + r
                s = 16 * w + 2 * r
                f2 = pltpu.roll(fr, BLK - s, 1) if s else fr
                lhs[cp, 0:BLK, :] = jnp.where(lane < 8, wt, jnp.where(lane < 16, f2, 0.0)).astype(BF)
                sh = (16 - 16 * r) % BLK
                b2 = pltpu.roll(wr, sh, 1) if sh else wr
                lhs[cp, BLK : 2 * BLK, :] = jnp.where(lane < 16, 0.0, b2).astype(BF)
                bt[cp] = bt32[16 * cp : 16 * cp + 16, :].astype(BF)

    for x in xs:
        rcopy(posx.at[GRP + x], posx.at[GRP + x], p_send.at[0], p_recv.at[GRP + x], (dm, x)).wait_recv()
        rcopy(meta.at[x], meta.at[x], m_send.at[0], m_recv.at[x], (dm, x)).wait_recv()
    for x in range(GRP):
        rcopy(posx.at[x], posx.at[x], p_send.at[0], p_recv.at[x], (dn, x)).wait_recv()
        rcopy(posx.at[2 * GRP + x], posx.at[2 * GRP + x], p_send.at[0], p_recv.at[2 * GRP + x], (up, x)).wait_recv()
    mc = pltpu.make_async_copy(meta, meta_sm, loc_sem)
    mc.start()
    mc.wait()
    pc = jnp.concatenate([posx[GRP + c] for c in range(GRP)] + [jnp.zeros((BLK - 8 * GRP, BLK), F32)], 0)
    ptr[...] = pc.T
    pq = ptr[pl.ds(pl.multiple_of(QTR * g, QTR), QTR), :]
    for c in range(GRP):
        for m in range(3):
            cposb[c, m] = jnp.broadcast_to(pq[:, 8 * c + m : 8 * c + m + 1], (QTR, BLK))

    col = lax.broadcasted_iota(jnp.int32, (8, BLK), 0)
    neg = jnp.zeros((8, BLK), F32)
    for b, rate in enumerate(RATES):
        neg = jnp.where(col == b, -rate, neg)
    half_neg = 0.5 * neg
    z8 = jnp.zeros((8, BLK), F32)
    one0 = jnp.where(sub8 == 0, 1.0, 0.0)
    one1 = jnp.where(sub8 == 1, 1.0, 0.0)

    def slot_of(t):
        gs = t // SLOTS
        ti = lax.rem(t, SLOTS)
        return meta_sm[gs, 0, ti], meta_sm[gs, 0, SLOTS + ti], gs, ti

    def geometry(t, carry):
        c, n, gs, ti = slot_of(t)
        row = posx[n]
        shift = (n // GRP - 1).astype(F32)
        selff = jnp.where(n == c + GRP, 1.0, 0.0)
        npos = [jnp.broadcast_to(row[m : m + 1, :], (8, BLK)) for m in range(3)]
        npos[2] = npos[2] + shift
        for q in range(QTR // 8):
            sl = slice(8 * q, 8 * q + 8)
            d = [npos[m] - cposb[c, m, sl, :] for m in range(3)]
            s2 = d[0] * d[0] + d[1] * d[1] + d[2] * d[2]
            keep = 1.0 - jnp.where(lane8 == sub8 + (QTR * g + 8 * q), selff, 0.0)
            inner = jnp.maximum(1.0 - s2 * 0.25, 0.0)
            env = inner * inner * keep
            s2_s[sl, :] = s2
            hd = [v * 0.5 for v in d]
            ys = [env] + [env * v for v in hd]
            for m in range(4):
                y_s[pl.ds(64 * q + m, 8, stride=8), :] = ys[m]
                y_s[pl.ds(64 * q + m + 4, 8, stride=8), :] = ys[m]
            for k, v in enumerate(hd + [env, inner * keep]):
                ds[t, k, sl, :] = v
        for r in range(PAIRS):
            p = t * PAIRS + r
            bs = []
            for e in range(2):
                b = jnp.exp(s2_s[pl.ds(2 * r + e, 8, stride=0), :] * neg)
                bas[2 * p + e] = b * half_neg
                bs.append(b)
            y0 = y_s[16 * r : 16 * r + 8, :]
            y1 = y_s[16 * r + 8 : 16 * r + 16, :]
            top = jnp.concatenate([jnp.concatenate([bs[0], one0], 0), jnp.concatenate([bs[1], one1], 0)], 1)
            low = jnp.concatenate([jnp.concatenate([y0, z8], 0), jnp.concatenate([z8, y1], 0)], 1)
            rhs[p, 0:16, :] = top.astype(BF)
            rhs[p, 16:32, :] = low.astype(BF)
        return carry

    lax.fori_loop(0, NSLOT, geometry, 0)

    def project(b):
        v = lax.dot_general(nw_in[...], featx[b], (((0,), (0,)), ((), ())), preferred_element_type=F32)
        nf[b] = v.astype(BF).astype(F32) * 0.5

    for c in range(GRP):
        project(GRP + c)
    for x in [g, *xs]:
        rcopy(featx.at[x], featx.at[x], fz_send.at[0], f_recv.at[x], (dn, g)).wait_recv()
        project(x)
        rcopy(featx.at[2 * GRP + x], featx.at[2 * GRP + x], fz_send.at[0], f_recv.at[2 * GRP + x], (up, g)).wait_recv()
        project(2 * GRP + x)

    zpad = jnp.zeros((96, 2 * BLK), BF)
    zbt = jnp.zeros((16, BLK), BF)

    def stage_a(c, n, r, p, buf):
        o = jnp.dot(lhs[c * PAIRS + r], jnp.concatenate([rhs[p], zpad], 0), preferred_element_type=F32)
        nn = nf[n]
        hb[buf, 0:BLK, :] = (o[:BLK] + jnp.concatenate([nn, nn], 1)).astype(BF)
        hb[buf, BLK : 2 * BLK, :] = o[BLK:].astype(BF)

    def stage_b(buf):
        for k in range(0, BLK, 16):
            hid, pg = pair_values(hb[buf, k : k + 16, :], hb[buf, BLK + k : BLK + k + 16, :])
            xb[buf, k : k + 16, :] = hid
            xb[buf, BLK + k : BLK + k + 16, :] = pg

    def stage_c(c, r, p, buf):
        lr = jnp.concatenate([jnp.concatenate([bt[c * PAIRS + r], zbt], 1), wred[...]], 0)
        o = jnp.dot(lr, xb[buf], preferred_element_type=F32)
        for e in range(2):
            cut = slice(BLK * e, BLK * e + BLK)
            al[2 * p + e] = o[8 * e : 8 * e + 8, cut]
            pr[2 * p + e] = o[16:24, cut] * bas[2 * p + e]

    def main(k, carry):
        ta = jnp.minimum(k, NSLOT - 1)
        tl = jnp.maximum(k - 1, 0)
        ca, na, _, _ = slot_of(ta)
        cl, _, _, _ = slot_of(tl)
        for half in range(2):
            for u in range(U):
                r = half * U + u
                stage_a(ca, na, r, ta * PAIRS + r, r)
                stage_b((1 - half) * U + u)
                stage_c(cl, r, tl * PAIRS + r, r)
        return carry

    lax.fori_loop(0, NSLOT + 1, main, 0)

    def finish(t, carry):
        c, n, gs, ti = slot_of(t)
        live = jnp.where(ti < meta_sm[gs, 0, 2 * SLOTS], 1.0, 0.0)
        ng = [jnp.zeros((8, BLK), F32)] * 3
        base = t * QTR
        for q in range(QTR // 8):
            sl = slice(8 * q, 8 * q + 8)
            at8 = pl.ds(base + 8 * q, 8)
            s = pr[at8, 0, :]
            for b in range(1, 8):
                s = s + pr[at8, b, :]
            av = [al[at8, m, :] + al[at8, m + 4, :] for m in range(4)]
            hd = [ds[t, k, sl, :] for k in range(3)]
            env = ds[t, 3, sl, :]
            ik = ds[t, 4, sl, :]
            eg = av[0] + av[1] * hd[0] + av[2] * hd[1] + av[3] * hd[2]
            sq = (s - 0.5 * eg * ik) * (4.0 * live)
            ev = env * (0.5 * live)
            for m in range(3):
                dg = sq * hd[m] + ev * av[m + 1]
                ng[m] = ng[m] + dg
                for k in range(GRP):
                    cacc[k, m, sl, :] += jnp.where(c == k, 1.0, 0.0) * dg
        v = jnp.concatenate([jnp.sum(a, axis=0, keepdims=True) for a in ng] + [jnp.zeros((5, BLK), F32)], 0)
        for k in range(3 * GRP):
            nacc[k] += jnp.where(n == k, 1.0, 0.0) * v
        return carry

    lax.fori_loop(0, NSLOT, finish, 0)

    crow = jnp.concatenate(
        [jnp.sum(cacc[:, m].reshape(BLK, BLK).T, axis=0, keepdims=True) for m in range(3)]
        + [jnp.zeros((5, BLK), F32)],
        0,
    )
    mine = (lane8 >= QTR * g) & (lane8 < QTR * g + QTR)
    for x in range(GRP):
        moved = pltpu.roll(crow, lax.rem(QTR * g + BLK - QTR * x, BLK), 1)
        res_send[x] = nacc[x]
        res_send[GRP + x] = nacc[GRP + x] - jnp.where(mine, moved, 0.0)
        res_send[2 * GRP + x] = nacc[2 * GRP + x]
    for j, x in enumerate(xs):
        go(rcopy(res_send.at[GRP + x], res_recv.at[own], r_send.at[j], r_recv.at[own], (dm, x)))
    for x in range(GRP):
        go(rcopy(res_send.at[x], res_recv.at[2 * GRP + g], r_send.at[3 + x], r_recv.at[2 * GRP + g], (dn, x)))
        go(rcopy(res_send.at[2 * GRP + x], res_recv.at[g], r_send.at[7 + x], r_recv.at[g], (up, x)))
    total = res_send[own]
    for x in xs:
        rcopy(res_recv.at[GRP + x], res_recv.at[GRP + x], r_send.at[0], r_recv.at[GRP + x], (dm, x)).wait_recv()
        total = total + res_recv[GRP + x]
    for x in range(GRP):
        rcopy(res_recv.at[x], res_recv.at[x], r_send.at[0], r_recv.at[x], (dn, x)).wait_recv()
        total = total + res_recv[x]
        rcopy(
            res_recv.at[2 * GRP + x], res_recv.at[2 * GRP + x], r_send.at[0], r_recv.at[2 * GRP + x], (up, x)
        ).wait_recv()
        total = total + res_recv[2 * GRP + x]
    out_ref[...] = total[0:3, :]
    for c in sends:
        c.wait_send()


def on_device(*args):
    V = pltpu.VMEM
    vs = pl.BlockSpec(memory_space=pltpu.VMEM)
    sm = pl.BlockSpec(memory_space=pltpu.SMEM)
    D = pltpu.SemaphoreType.DMA
    return pl.pallas_call(
        body,
        out_shape=jax.ShapeDtypeStruct((3, BLK), F32),
        in_specs=[vs] * 6 + [sm] * 3,
        out_specs=vs,
        scratch_shapes=[
            V((3 * GRP, BLK, BLK), BF),
            V((3 * GRP, 8, BLK), F32),
            V((GRP, 8, BLK), jnp.int32),
            pltpu.SMEM((GRP, 8, BLK), jnp.int32),
            V((BLK, 256), BF),
            V((GRP, QTR, 256), BF),
            V((3 * GRP, 8, BLK), F32),
            V((3 * GRP, 8, BLK), F32),
            V((3 * GRP, BLK, BLK), F32),
            V((BLK, BLK), F32),
            V((GRP, 3, QTR, BLK), F32),
            V((8 * BLK, BLK), F32),
            V((GRP * PAIRS, 16, BLK), BF),
            V((GRP * PAIRS, 2 * BLK, BLK), BF),
            V((16, 2 * BLK), BF),
            V((NSLOT * PAIRS, 32, 2 * BLK), BF),
            V((NSLOT * QTR, 8, BLK), F32),
            V((NSLOT * QTR, 8, BLK), F32),
            V((NSLOT * QTR, 8, BLK), F32),
            V((NSLOT, 5, QTR, BLK), F32),
            V((8 * QTR, BLK), F32),
            V((QTR, BLK), F32),
            V((3 * GRP, 8, BLK), F32),
            V((GRP, 3, QTR, BLK), F32),
            V((2 * U, 2 * BLK, 2 * BLK), BF),
            V((2 * U, 2 * BLK, 2 * BLK), BF),
            D((3,)),
            D((8,)),
            D((12,)),
            D((3,)),
            D((4,)),
            D((11,)),
            D((12,)),
            D((3,)),
            D((4,)),
            D((11,)),
            D((12,)),
            D,
        ],
        compiler_params=pltpu.CompilerParams(collective_id=0, has_side_effects=True),
        name="allegro_forces",
    )(*args)


def solution(mesh):
    placed = (
        P(None, ("dom", "grp")),
        P(None, ("dom", "grp")),
        P(),
        P(None, ("dom", "grp")),
        P(),
        P(),
        P(("dom", "grp")),
        P(("dom", "grp")),
        P(("dom", "grp")),
    )
    return jax.shard_map(
        on_device, mesh=mesh, in_specs=placed, out_specs=P(None, ("dom", "grp")), check_vma=False
    )
```

```python
import jax
import jax.numpy as jnp
from jax import lax
from jax.experimental import pallas as pl
from jax.experimental.pallas import tpu as pltpu
from jax.sharding import PartitionSpec as P

BF = jnp.bfloat16
F32 = jnp.float32
BLK = 128
GRP = 4
SLOTS = 4
NSLOT = GRP * SLOTS
QTR = BLK // GRP
PAIRS = QTR // 2
MESH = pl.DeviceIdType.MESH

RATES = tuple(0.3 * 1.5**b for b in range(8))


def pair_values(h, hg):
    one = jnp.asarray(1.0, BF)
    t = jnp.tanh(h)
    p = one + t
    hid = h * p
    return hid, hg * (p + hid * (one - t))


def body(
    pos_in, feat_in, nw_in, adj_in, bw_in, ew_in, tc_in, tn_in, cnt_in, out_ref,
    featx, posx, meta, meta_sm, at_send, at_all, res_send, res_recv,
    nf, ptr, cposb, bt32, bt, lp, lh, oneh, wred, rhs, bas, al, pr, ds, y_s, s2_s, nacc, cacc,
    hb, xb,
    fx_send, fz_send, f_recv, a_send, a_recv, p_send, p_recv, m_send, m_recv,
    r_send, r_recv, loc_sem,
):
    g = lax.axis_index("grp")
    dm = lax.axis_index("dom")
    n_dom = lax.axis_size("dom")
    up = lax.rem(dm + 1, n_dom)
    dn = lax.rem(dm + n_dom - 1, n_dom)
    xs = [lax.rem(g + j, GRP) for j in range(1, GRP)]
    barrier = pltpu.get_barrier_semaphore()
    for x in xs:
        pl.semaphore_signal(barrier, inc=1, device_id=(dm, x), device_id_type=MESH)
    for d in (up, dn):
        for x in range(GRP):
            pl.semaphore_signal(barrier, inc=1, device_id=(d, x), device_id_type=MESH)

    lane8 = lax.broadcasted_iota(jnp.int32, (8, BLK), 1)
    sub8 = lax.broadcasted_iota(jnp.int32, (8, BLK), 0)
    mv = jnp.zeros((8, BLK), jnp.int32)
    for t in range(SLOTS):
        mv = jnp.where(lane8 == t, tc_in[t], mv)
        mv = jnp.where(lane8 == SLOTS + t, tn_in[t], mv)
    meta[g] = jnp.where(lane8 == 2 * SLOTS, cnt_in[0], mv)
    posx[GRP + g] = jnp.concatenate([pos_in[...], jnp.zeros((5, BLK), F32)], 0)
    at_send[...] = adj_in[...].astype(F32).T.astype(BF)

    pl.semaphore_wait(barrier, 11)

    def rcopy(src, dst, ss, rs, dev):
        return pltpu.make_async_remote_copy(
            src_ref=src, dst_ref=dst, send_sem=ss, recv_sem=rs, device_id=dev, device_id_type=MESH
        )

    sends = []

    def go(c):
        c.start()
        sends.append(c)

    own = GRP + g
    for j, x in enumerate(xs):
        go(rcopy(posx.at[own], posx.at[own], p_send.at[j], p_recv.at[own], (dm, x)))
        go(rcopy(meta.at[g], meta.at[g], m_send.at[j], m_recv.at[g], (dm, x)))
    for x in range(GRP):
        go(rcopy(posx.at[own], posx.at[g], p_send.at[3 + x], p_recv.at[g], (up, x)))
        go(rcopy(posx.at[own], posx.at[2 * GRP + g], p_send.at[7 + x], p_recv.at[2 * GRP + g], (dn, x)))
    for j, x in enumerate(xs):
        rows = pl.ds(pl.multiple_of(QTR * x, QTR), QTR)
        go(rcopy(at_send.at[rows, :], at_all.at[g], a_send.at[j], a_recv.at[g], (dm, x)))
    for j, x in enumerate((xs[0], xs[2], xs[1])):
        go(rcopy(feat_in, featx.at[own], fx_send.at[j], f_recv.at[own], (dm, x)))
    go(rcopy(feat_in, featx.at[g], fz_send.at[0], f_recv.at[g], (up, g)))
    go(rcopy(feat_in, featx.at[2 * GRP + g], fz_send.at[1], f_recv.at[2 * GRP + g], (dn, g)))

    featx[own] = feat_in[...]
    at_all[g] = at_send[pl.ds(pl.multiple_of(QTR * g, QTR), QTR), :]
    wred[...] = jnp.concatenate(
        [
            jnp.concatenate([jnp.zeros((8, BLK), F32), bw_in[...].astype(F32)], 1),
            jnp.zeros((8, 2 * BLK), F32),
        ],
        0,
    ).astype(BF)
    nacc[...] = jnp.zeros_like(nacc)
    cacc[...] = jnp.zeros_like(cacc)

    for x in xs:
        rcopy(at_all.at[x], at_all.at[x], a_send.at[0], a_recv.at[x], (dm, x)).wait_recv()
    at2 = at_all[...].reshape(BLK, 4 * 64)
    for m in range(4):
        bm = lax.dot_general(
            at2[:, 64 * m : 64 * m + 64], ew_in[...], (((1,), (0,)), ((), ())), preferred_element_type=F32
        )
        hi = bm.astype(BF).astype(F32)
        bt32[pl.ds(m, BLK, stride=8), :] = hi
        bt32[pl.ds(4 + m, BLK, stride=8), :] = bm - hi

    for j, x in enumerate((xs[0], xs[2], xs[1])):
        blk = GRP + x
        rcopy(featx.at[blk], featx.at[blk], fx_send.at[0], f_recv.at[blk], (dm, x)).wait_recv()
        go(rcopy(featx.at[blk], featx.at[x], fz_send.at[2 + 2 * j], f_recv.at[x], (up, g)))
        go(rcopy(featx.at[blk], featx.at[2 * GRP + x], fz_send.at[3 + 2 * j], f_recv.at[2 * GRP + x], (dn, g)))

    lane = lax.broadcasted_iota(jnp.int32, (BLK, BLK), 1)
    wt = (
        jnp.concatenate([bw_in[...].astype(F32), jnp.zeros((BLK - 8, BLK), F32)], 0).T * 0.5
    )
    for c in range(GRP):
        fr = pltpu.roll(featx[GRP + c].astype(F32) * 0.5, lax.rem(16 + BLK - QTR * g, BLK), 1)
        for w in range(2):
            f2 = pltpu.roll(fr, BLK - 16, 1) if w else fr
            lp[2 * c + w] = jnp.where(lane < 8, wt, jnp.where(lane < 16, 0.0, f2)).astype(BF)
            lh[2 * c + w] = bt32[BLK * (2 * c + w) : BLK * (2 * c + w + 1), :].T.astype(BF)
    for cp in range(GRP * PAIRS):
        bt[cp] = bt32[16 * cp : 16 * cp + 16, :].astype(BF)
    row16 = lax.broadcasted_iota(jnp.int32, (16, 2 * BLK), 0)
    side = lax.broadcasted_iota(jnp.int32, (16, 2 * BLK), 1) // BLK
    for r in range(8):
        oneh[r] = jnp.where(row16 == 2 * r + side, 1.0, 0.0).astype(BF)

    for x in xs:
        rcopy(posx.at[GRP + x], posx.at[GRP + x], p_send.at[0], p_recv.at[GRP + x], (dm, x)).wait_recv()
        rcopy(meta.at[x], meta.at[x], m_send.at[0], m_recv.at[x], (dm, x)).wait_recv()
    for x in range(GRP):
        rcopy(posx.at[x], posx.at[x], p_send.at[0], p_recv.at[x], (dn, x)).wait_recv()
        rcopy(posx.at[2 * GRP + x], posx.at[2 * GRP + x], p_send.at[0], p_recv.at[2 * GRP + x], (up, x)).wait_recv()
    mc = pltpu.make_async_copy(meta, meta_sm, loc_sem)
    mc.start()
    mc.wait()
    pc = jnp.concatenate([posx[GRP + c] for c in range(GRP)] + [jnp.zeros((BLK - 8 * GRP, BLK), F32)], 0)
    ptr[...] = pc.T
    pq = ptr[pl.ds(pl.multiple_of(QTR * g, QTR), QTR), :]
    for c in range(GRP):
        for m in range(3):
            cposb[c, m] = jnp.broadcast_to(pq[:, 8 * c + m : 8 * c + m + 1], (QTR, BLK))

    col = lax.broadcasted_iota(jnp.int32, (8, BLK), 0)
    neg = jnp.zeros((8, BLK), F32)
    for b, rate in enumerate(RATES):
        neg = jnp.where(col == b, -rate, neg)
    half_neg = 0.5 * neg
    z8 = jnp.zeros((8, BLK), F32)

    def slot_of(t):
        gs = t // SLOTS
        ti = lax.rem(t, SLOTS)
        return meta_sm[gs, 0, ti], meta_sm[gs, 0, SLOTS + ti], gs, ti

    def geometry(t, carry):
        c, n, gs, ti = slot_of(t)
        row = posx[n]
        shift = (n // GRP - 1).astype(F32)
        selff = jnp.where(n == c + GRP, 1.0, 0.0)
        npos = [jnp.broadcast_to(row[m : m + 1, :], (8, BLK)) for m in range(3)]
        npos[2] = npos[2] + shift
        for q in range(QTR // 8):
            sl = slice(8 * q, 8 * q + 8)
            d = [npos[m] - cposb[c, m, sl, :] for m in range(3)]
            s2 = d[0] * d[0] + d[1] * d[1] + d[2] * d[2]
            keep = 1.0 - jnp.where(lane8 == sub8 + (QTR * g + 8 * q), selff, 0.0)
            inner = jnp.maximum(1.0 - s2 * 0.25, 0.0)
            env = inner * inner * keep
            s2_s[sl, :] = s2
            hd = [v * 0.5 for v in d]
            ys = [env] + [env * v for v in hd]
            for m in range(4):
                y_s[pl.ds(64 * q + m, 8, stride=8), :] = ys[m]
                y_s[pl.ds(64 * q + m + 4, 8, stride=8), :] = ys[m]
            for k, v in enumerate(hd + [env, inner * keep]):
                ds[t, k, sl, :] = v
        for r in range(PAIRS):
            p = t * PAIRS + r
            bs = []
            for e in range(2):
                b = jnp.exp(s2_s[pl.ds(2 * r + e, 8, stride=0), :] * neg)
                bas[2 * p + e] = b * half_neg
                bs.append(b)
            y0 = y_s[16 * r : 16 * r + 8, :]
            y1 = y_s[16 * r + 8 : 16 * r + 16, :]
            top = jnp.concatenate([jnp.concatenate([bs[0], z8], 0), jnp.concatenate([bs[1], z8], 0)], 1)
            low = jnp.concatenate([jnp.concatenate([y0, z8], 0), jnp.concatenate([z8, y1], 0)], 1)
            rhs[p, 0:16, :] = top.astype(BF)
            rhs[p, 16:32, :] = low.astype(BF)
        return carry

    lax.fori_loop(0, NSLOT, geometry, 0)

    def project(b):
        v = lax.dot_general(nw_in[...], featx[b], (((0,), (0,)), ((), ())), preferred_element_type=F32)
        nf[b] = v.astype(BF).astype(F32) * 0.5

    for c in range(GRP):
        project(GRP + c)
    for x in [g, *xs]:
        rcopy(featx.at[x], featx.at[x], fz_send.at[0], f_recv.at[x], (dn, g)).wait_recv()
        project(x)
        rcopy(featx.at[2 * GRP + x], featx.at[2 * GRP + x], fz_send.at[0], f_recv.at[2 * GRP + x], (up, g)).wait_recv()
        project(2 * GRP + x)

    zrow = jnp.zeros((16, 2 * BLK), BF)
    zbt = jnp.zeros((16, BLK), BF)

    def stage_a(c, n, r, p):
        w, e = divmod(r, 8)
        right = jnp.concatenate([rhs[p, 0:16, :], oneh[e]] + [zrow] * 6, 0)
        h = jnp.dot(lp[2 * c + w], right, preferred_element_type=F32)
        nn = nf[n]
        hb[r, 0:BLK, :] = (h + jnp.concatenate([nn, nn], 1)).astype(BF)
        right = jnp.concatenate([zrow] * e + [rhs[p, 16:32, :]] + [zrow] * (7 - e), 0)
        hb[r, BLK : 2 * BLK, :] = jnp.dot(lh[2 * c + w], right, preferred_element_type=F32).astype(BF)

    def stage_b(r):
        for k in range(0, BLK, 16):
            hid, pg = pair_values(hb[r, k : k + 16, :], hb[r, BLK + k : BLK + k + 16, :])
            xb[r, k : k + 16, :] = hid
            xb[r, BLK + k : BLK + k + 16, :] = pg

    def stage_c(c, r, p):
        lr = jnp.concatenate([jnp.concatenate([bt[c * PAIRS + r], zbt], 1), wred[...]], 0)
        o = jnp.dot(lr, xb[r], preferred_element_type=F32)
        for e in range(2):
            i = 2 * r + e
            cut = slice(BLK * e, BLK * e + BLK)
            al[8 * i : 8 * i + 8, :] = o[8 * e : 8 * e + 8, cut]
            pr[8 * i : 8 * i + 8, :] = o[16:24, cut] * bas[2 * p + e]

    def finish(t, ready):
        c, n, gs, ti = slot_of(t)
        live = jnp.logical_and(ti < meta_sm[gs, 0, 2 * SLOTS], ready)
        ng = [jnp.zeros((8, BLK), F32)] * 3
        for q in range(QTR // 8):
            sl = slice(8 * q, 8 * q + 8)

            def strip(ref, k):
                return ref[pl.ds(64 * q + k, 8, stride=8), :]

            s = strip(pr, 0)
            for b in range(1, 8):
                s = s + strip(pr, b)
            av = [strip(al, m) + strip(al, m + 4) for m in range(4)]
            hd = [ds[t, k, sl, :] for k in range(3)]
            env = ds[t, 3, sl, :]
            ik = ds[t, 4, sl, :]
            eg = av[0] + av[1] * hd[0] + av[2] * hd[1] + av[3] * hd[2]
            sq = (s - 0.5 * eg * ik) * 4.0
            ev = env * 0.5
            for m in range(3):
                dg = jnp.where(live, sq * hd[m] + ev * av[m + 1], 0.0)
                ng[m] = ng[m] + dg
                for k in range(GRP):
                    cacc[k, m, sl, :] += jnp.where(c == k, 1.0, 0.0) * dg
        v = jnp.concatenate([jnp.sum(a, axis=0, keepdims=True) for a in ng] + [jnp.zeros((5, BLK), F32)], 0)
        for k in range(3 * GRP):
            nacc[k] += jnp.where(n == k, 1.0, 0.0) * v

    def first(c):
        return c[0], c[1]

    ca, na = first(slot_of(0))
    for r in range(PAIRS):
        stage_a(ca, na, r, r)

    def main(k, carry):
        ca, na = first(slot_of(k))
        tc = jnp.maximum(k - 2, 0)
        cc, _ = first(slot_of(tc))
        finish(jnp.maximum(k - 3, 0), k >= 3)
        for r in range(PAIRS):
            stage_c(cc, r, tc * PAIRS + r)
            stage_b(r)
            stage_a(ca, na, r, k * PAIRS + r)
        return carry

    lax.fori_loop(1, NSLOT, main, 0)
    last = NSLOT - 1
    finish(last - 2, True)
    cc, _ = first(slot_of(last - 1))
    for r in range(PAIRS):
        stage_c(cc, r, (last - 1) * PAIRS + r)
        stage_b(r)
    finish(last - 1, True)
    cc, _ = first(slot_of(last))
    for r in range(PAIRS):
        stage_c(cc, r, last * PAIRS + r)
    finish(last, True)

    crow = jnp.concatenate(
        [jnp.sum(cacc[:, m].reshape(BLK, BLK).T, axis=0, keepdims=True) for m in range(3)]
        + [jnp.zeros((5, BLK), F32)],
        0,
    )
    mine = (lane8 >= QTR * g) & (lane8 < QTR * g + QTR)
    for x in range(GRP):
        moved = pltpu.roll(crow, lax.rem(QTR * g + BLK - QTR * x, BLK), 1)
        res_send[x] = nacc[x]
        res_send[GRP + x] = nacc[GRP + x] - jnp.where(mine, moved, 0.0)
        res_send[2 * GRP + x] = nacc[2 * GRP + x]
    for j, x in enumerate(xs):
        go(rcopy(res_send.at[GRP + x], res_recv.at[own], r_send.at[j], r_recv.at[own], (dm, x)))
    for x in range(GRP):
        go(rcopy(res_send.at[x], res_recv.at[2 * GRP + g], r_send.at[3 + x], r_recv.at[2 * GRP + g], (dn, x)))
        go(rcopy(res_send.at[2 * GRP + x], res_recv.at[g], r_send.at[7 + x], r_recv.at[g], (up, x)))
    out_ref[0] = res_send[own][0:3, :]
    total = jnp.zeros((8, BLK), F32)
    for x in xs:
        rcopy(res_recv.at[GRP + x], res_recv.at[GRP + x], r_send.at[0], r_recv.at[GRP + x], (dm, x)).wait_recv()
        total = total + res_recv[GRP + x]
    for x in range(GRP):
        rcopy(res_recv.at[x], res_recv.at[x], r_send.at[0], r_recv.at[x], (dn, x)).wait_recv()
        total = total + res_recv[x]
        rcopy(
            res_recv.at[2 * GRP + x], res_recv.at[2 * GRP + x], r_send.at[0], r_recv.at[2 * GRP + x], (up, x)
        ).wait_recv()
        total = total + res_recv[2 * GRP + x]
    out_ref[1] = total[0:3, :]
    for c in sends:
        c.wait_send()


def on_device(pos, feat, nw, adj, bw, ew, tc, tn, cnt):
    V = pltpu.VMEM
    vs = pl.BlockSpec(memory_space=pltpu.VMEM)
    sm = pl.BlockSpec(memory_space=pltpu.SMEM)
    D = pltpu.SemaphoreType.DMA
    parts = pl.pallas_call(
        body,
        out_shape=jax.ShapeDtypeStruct((2, 3, BLK), F32),
        in_specs=[vs] * 6 + [sm] * 3,
        out_specs=vs,
        scratch_shapes=[
            V((3 * GRP, BLK, BLK), BF),
            V((3 * GRP, 8, BLK), F32),
            V((GRP, 8, BLK), jnp.int32),
            pltpu.SMEM((GRP, 8, BLK), jnp.int32),
            V((BLK, 256), BF),
            V((GRP, QTR, 256), BF),
            V((3 * GRP, 8, BLK), F32),
            V((3 * GRP, 8, BLK), F32),
            V((3 * GRP, BLK, BLK), F32),
            V((BLK, BLK), F32),
            V((GRP, 3, QTR, BLK), F32),
            V((8 * BLK, BLK), F32),
            V((GRP * PAIRS, 16, BLK), BF),
            V((2 * GRP, BLK, BLK), BF),
            V((2 * GRP, BLK, BLK), BF),
            V((8, 16, 2 * BLK), BF),
            V((16, 2 * BLK), BF),
            V((NSLOT * PAIRS, 32, 2 * BLK), BF),
            V((NSLOT * QTR, 8, BLK), F32),
            V((8 * QTR, BLK), F32),
            V((8 * QTR, BLK), F32),
            V((NSLOT, 5, QTR, BLK), F32),
            V((8 * QTR, BLK), F32),
            V((QTR, BLK), F32),
            V((3 * GRP, 8, BLK), F32),
            V((GRP, 3, QTR, BLK), F32),
            V((PAIRS, 2 * BLK, 2 * BLK), BF),
            V((PAIRS, 2 * BLK, 2 * BLK), BF),
            D((3,)),
            D((8,)),
            D((12,)),
            D((3,)),
            D((4,)),
            D((11,)),
            D((12,)),
            D((3,)),
            D((4,)),
            D((11,)),
            D((12,)),
            D,
        ],
        compiler_params=pltpu.CompilerParams(collective_id=0, has_side_effects=True),
        name="allegro_forces",
    )(pos, feat, nw, adj, bw, ew.T, tc, tn, cnt)
    return parts[0] + parts[1]


def solution(mesh):
    placed = (
        P(None, ("dom", "grp")),
        P(None, ("dom", "grp")),
        P(),
        P(None, ("dom", "grp")),
        P(),
        P(),
        P(("dom", "grp")),
        P(("dom", "grp")),
        P(("dom", "grp")),
    )
    return jax.shard_map(
        on_device, mesh=mesh, in_specs=placed, out_specs=P(None, ("dom", "grp")), check_vma=False
    )
```

```python
import jax
import jax.numpy as jnp
from jax import lax
from jax.experimental import pallas as pl
from jax.experimental.pallas import tpu as pltpu
from jax.sharding import PartitionSpec as P

BF = jnp.bfloat16
F32 = jnp.float32
BLK = 128
GRP = 4
SLOTS = 4
NSLOT = GRP * SLOTS
QTR = BLK // GRP
PAIRS = QTR // 2
MESH = pl.DeviceIdType.MESH

RATES = tuple(0.3 * 1.5**b for b in range(8))


def pair_values(h):
    one = jnp.asarray(1.0, BF)
    t = jnp.tanh(h)
    p = one + t
    hid = h * p
    return hid, p + hid * (one - t)


def body(
    pos_in, feat_in, nw_in, adj_in, bw_in, ew_in, tc_in, tn_in, cnt_in, out_ref,
    featx, posx, meta, meta_sm, at_send, at_all, res_send, res_recv,
    nf, ptr, cposb, bt32, bmf, bt, wb, lp, oneh, rhs, bas, al, pr, ds, y_all, s2_s, nacc, cacc,
    hb, xb,
    fx_send, fz_send, f_recv, a_send, a_recv, p_send, p_recv, m_send, m_recv,
    r_send, r_recv, loc_sem,
):
    g = lax.axis_index("grp")
    dm = lax.axis_index("dom")
    n_dom = lax.axis_size("dom")
    up = lax.rem(dm + 1, n_dom)
    dn = lax.rem(dm + n_dom - 1, n_dom)
    xs = [lax.rem(g + j, GRP) for j in range(1, GRP)]
    barrier = pltpu.get_barrier_semaphore()
    for x in xs:
        pl.semaphore_signal(barrier, inc=1, device_id=(dm, x), device_id_type=MESH)
    for d in (up, dn):
        for x in range(GRP):
            pl.semaphore_signal(barrier, inc=1, device_id=(d, x), device_id_type=MESH)

    lane8 = lax.broadcasted_iota(jnp.int32, (8, BLK), 1)
    sub8 = lax.broadcasted_iota(jnp.int32, (8, BLK), 0)
    mv = jnp.zeros((8, BLK), jnp.int32)
    for t in range(SLOTS):
        mv = jnp.where(lane8 == t, tc_in[t], mv)
        mv = jnp.where(lane8 == SLOTS + t, tn_in[t], mv)
    meta[g] = jnp.where(lane8 == 2 * SLOTS, cnt_in[0], mv)
    posx[GRP + g] = jnp.concatenate([pos_in[...], jnp.zeros((5, BLK), F32)], 0)
    at_send[...] = adj_in[...].astype(F32).T.astype(BF)

    pl.semaphore_wait(barrier, 11)

    def rcopy(src, dst, ss, rs, dev):
        return pltpu.make_async_remote_copy(
            src_ref=src, dst_ref=dst, send_sem=ss, recv_sem=rs, device_id=dev, device_id_type=MESH
        )

    sends = []

    def go(c):
        c.start()
        sends.append(c)

    own = GRP + g
    for j, x in enumerate(xs):
        go(rcopy(posx.at[own], posx.at[own], p_send.at[j], p_recv.at[own], (dm, x)))
        go(rcopy(meta.at[g], meta.at[g], m_send.at[j], m_recv.at[g], (dm, x)))
    for x in range(GRP):
        go(rcopy(posx.at[own], posx.at[g], p_send.at[3 + x], p_recv.at[g], (up, x)))
        go(rcopy(posx.at[own], posx.at[2 * GRP + g], p_send.at[7 + x], p_recv.at[2 * GRP + g], (dn, x)))
    for j, x in enumerate(xs):
        rows = pl.ds(pl.multiple_of(QTR * x, QTR), QTR)
        go(rcopy(at_send.at[rows, :], at_all.at[g], a_send.at[j], a_recv.at[g], (dm, x)))
    for j, x in enumerate((xs[0], xs[2], xs[1])):
        go(rcopy(feat_in, featx.at[own], fx_send.at[j], f_recv.at[own], (dm, x)))
    go(rcopy(feat_in, featx.at[g], fz_send.at[0], f_recv.at[g], (up, g)))
    go(rcopy(feat_in, featx.at[2 * GRP + g], fz_send.at[1], f_recv.at[2 * GRP + g], (dn, g)))

    featx[own] = feat_in[...]
    at_all[g] = at_send[pl.ds(pl.multiple_of(QTR * g, QTR), QTR), :]
    nacc[...] = jnp.zeros_like(nacc)
    cacc[...] = jnp.zeros_like(cacc)

    for x in xs:
        rcopy(at_all.at[x], at_all.at[x], a_send.at[0], a_recv.at[x], (dm, x)).wait_recv()
    at2 = at_all[...].reshape(BLK, 4 * 64)
    for m in range(4):
        bm = lax.dot_general(
            at2[:, 64 * m : 64 * m + 64], ew_in[...], (((1,), (0,)), ((), ())), preferred_element_type=F32
        )
        hi = bm.astype(BF).astype(F32)
        bt32[pl.ds(m, BLK, stride=8), :] = hi
        bt32[pl.ds(4 + m, BLK, stride=8), :] = bm - hi
        bmf[BLK * m : BLK * m + BLK, :] = bm

    for j, x in enumerate((xs[0], xs[2], xs[1])):
        blk = GRP + x
        rcopy(featx.at[blk], featx.at[blk], fx_send.at[0], f_recv.at[blk], (dm, x)).wait_recv()
        go(rcopy(featx.at[blk], featx.at[x], fz_send.at[2 + 2 * j], f_recv.at[x], (up, g)))
        go(rcopy(featx.at[blk], featx.at[2 * GRP + x], fz_send.at[3 + 2 * j], f_recv.at[2 * GRP + x], (dn, g)))

    lane = lax.broadcasted_iota(jnp.int32, (BLK, BLK), 1)
    wt = (
        jnp.concatenate([bw_in[...].astype(F32), jnp.zeros((BLK - 8, BLK), F32)], 0).T * 0.5
    )
    for c in range(GRP):
        fr = pltpu.roll(featx[GRP + c].astype(F32) * 0.5, lax.rem(16 + BLK - QTR * g, BLK), 1)
        for w in range(2):
            f2 = pltpu.roll(fr, BLK - 16, 1) if w else fr
            lp[2 * c + w] = jnp.where(lane < 8, wt, jnp.where(lane < 16, 0.0, f2)).astype(BF)
    bwf = bw_in[...].astype(F32)

    def centre_rows(cp, carry):
        bt[cp] = bt32[pl.ds(pl.multiple_of(16 * cp, 16), 16), :].astype(BF)
        for e in range(2):
            v = [bmf[pl.ds(BLK * m + 2 * cp + e, 8, stride=0), :] * bwf for m in range(4)]
            wb[cp, 32 * e : 32 * e + 32, :] = jnp.concatenate(v, 0).astype(BF)
        return carry

    lax.fori_loop(0, GRP * PAIRS, centre_rows, 0, unroll=8)
    row16 = lax.broadcasted_iota(jnp.int32, (16, 2 * BLK), 0)
    side = lax.broadcasted_iota(jnp.int32, (16, 2 * BLK), 1) // BLK
    for r in range(8):
        oneh[r] = jnp.where(row16 == 2 * r + side, 1.0, 0.0).astype(BF)

    for x in xs:
        rcopy(posx.at[GRP + x], posx.at[GRP + x], p_send.at[0], p_recv.at[GRP + x], (dm, x)).wait_recv()
        rcopy(meta.at[x], meta.at[x], m_send.at[0], m_recv.at[x], (dm, x)).wait_recv()
    for x in range(GRP):
        rcopy(posx.at[x], posx.at[x], p_send.at[0], p_recv.at[x], (dn, x)).wait_recv()
        rcopy(posx.at[2 * GRP + x], posx.at[2 * GRP + x], p_send.at[0], p_recv.at[2 * GRP + x], (up, x)).wait_recv()
    mc = pltpu.make_async_copy(meta, meta_sm, loc_sem)
    mc.start()
    mc.wait()
    pc = jnp.concatenate([posx[GRP + c] for c in range(GRP)] + [jnp.zeros((BLK - 8 * GRP, BLK), F32)], 0)
    ptr[...] = pc.T
    pq = ptr[pl.ds(pl.multiple_of(QTR * g, QTR), QTR), :]
    for c in range(GRP):
        for m in range(3):
            cposb[c, m] = jnp.broadcast_to(pq[:, 8 * c + m : 8 * c + m + 1], (QTR, BLK))

    col = lax.broadcasted_iota(jnp.int32, (8, BLK), 0)
    neg = jnp.zeros((8, BLK), F32)
    for b, rate in enumerate(RATES):
        neg = jnp.where(col == b, -rate, neg)
    half_neg = 0.5 * neg
    z8 = jnp.zeros((8, BLK), F32)

    def slot_of(t):
        gs = t // SLOTS
        ti = lax.rem(t, SLOTS)
        return meta_sm[gs, 0, ti], meta_sm[gs, 0, SLOTS + ti], gs, ti

    def geometry(t, carry):
        c, n, gs, ti = slot_of(t)
        row = posx[n]
        shift = (n // GRP - 1).astype(F32)
        selff = jnp.where(n == c + GRP, 1.0, 0.0)
        npos = [jnp.broadcast_to(row[m : m + 1, :], (8, BLK)) for m in range(3)]
        npos[2] = npos[2] + shift
        for q in range(QTR // 8):
            sl = slice(8 * q, 8 * q + 8)
            d = [npos[m] - cposb[c, m, sl, :] for m in range(3)]
            s2 = d[0] * d[0] + d[1] * d[1] + d[2] * d[2]
            keep = 1.0 - jnp.where(lane8 == sub8 + (QTR * g + 8 * q), selff, 0.0)
            inner = jnp.maximum(1.0 - s2 * 0.25, 0.0)
            env = inner * inner * keep
            s2_s[sl, :] = s2
            hd = [v * 0.5 for v in d]
            ys = [env] + [env * v for v in hd]
            for m in range(4):
                y_all[pl.ds(4 * QTR * t + 32 * q + m, 8, stride=4), :] = ys[m]
            for k, v in enumerate(hd + [env, inner * keep]):
                ds[t, k, sl, :] = v
        for r in range(PAIRS):
            p = t * PAIRS + r
            bs = []
            for e in range(2):
                b = jnp.exp(s2_s[pl.ds(2 * r + e, 8, stride=0), :] * neg)
                bas[2 * p + e] = b * half_neg
                bs.append(b)
            top = jnp.concatenate([jnp.concatenate([bs[0], z8], 0), jnp.concatenate([bs[1], z8], 0)], 1)
            rhs[p] = top.astype(BF)
        return carry

    lax.fori_loop(0, NSLOT, geometry, 0)

    def project(b):
        v = lax.dot_general(nw_in[...], featx[b], (((0,), (0,)), ((), ())), preferred_element_type=F32)
        nf[b] = v.astype(BF).astype(F32) * 0.5

    for c in range(GRP):
        project(GRP + c)
    for x in [g, *xs]:
        rcopy(featx.at[x], featx.at[x], fz_send.at[0], f_recv.at[x], (dn, g)).wait_recv()
        project(x)
        rcopy(featx.at[2 * GRP + x], featx.at[2 * GRP + x], fz_send.at[0], f_recv.at[2 * GRP + x], (up, g)).wait_recv()
        project(2 * GRP + x)

    zrow = jnp.zeros((16, 2 * BLK), BF)
    zbt = jnp.zeros((16, BLK), BF)

    def stage_a(c, n, r, p):
        w, e = divmod(r, 8)
        right = jnp.concatenate([rhs[p], oneh[e]] + [zrow] * 6, 0)
        h = jnp.dot(lp[2 * c + w], right, preferred_element_type=F32)
        nn = nf[n]
        hb[r] = (h + jnp.concatenate([nn, nn], 1)).astype(BF)

    def stage_b(r):
        for k in range(0, BLK, 16):
            hid, der = pair_values(hb[r, k : k + 16, :])
            xb[r, k : k + 16, :] = hid
            xb[r, BLK + k : BLK + k + 16, :] = der

    def stage_c(c, r, p):
        cp = c * PAIRS + r
        lr = jnp.concatenate(
            [jnp.concatenate([bt[cp], zbt], 1), jnp.concatenate([jnp.zeros((64, BLK), BF), wb[cp]], 1)], 0
        )
        o = jnp.dot(lr, xb[r], preferred_element_type=F32)
        for e in range(2):
            i = 2 * r + e
            cut = slice(BLK * e, BLK * e + BLK)
            al[8 * i : 8 * i + 8, :] = o[8 * e : 8 * e + 8, cut]
            first_row = 16 + 32 * e
            v = None
            for m in range(4):
                ym = y_all[pl.ds(4 * (2 * p + e) + m, 8, stride=0), :]
                w = ym * o[first_row + 8 * m : first_row + 8 * m + 8, cut]
                v = w if v is None else v + w
            pr[8 * i : 8 * i + 8, :] = v * bas[2 * p + e]

    def finish(t, ready):
        c, n, gs, ti = slot_of(t)
        live = jnp.logical_and(ti < meta_sm[gs, 0, 2 * SLOTS], ready)
        ng = [jnp.zeros((8, BLK), F32)] * 3
        for q in range(QTR // 8):
            sl = slice(8 * q, 8 * q + 8)

            def strip(ref, k):
                return ref[pl.ds(64 * q + k, 8, stride=8), :]

            s = strip(pr, 0)
            for b in range(1, 8):
                s = s + strip(pr, b)
            av = [strip(al, m) + strip(al, m + 4) for m in range(4)]
            hd = [ds[t, k, sl, :] for k in range(3)]
            env = ds[t, 3, sl, :]
            ik = ds[t, 4, sl, :]
            eg = av[0] + av[1] * hd[0] + av[2] * hd[1] + av[3] * hd[2]
            sq = (s - 0.5 * eg * ik) * 4.0
            ev = env * 0.5
            for m in range(3):
                dg = jnp.where(live, sq * hd[m] + ev * av[m + 1], 0.0)
                ng[m] = ng[m] + dg
                for k in range(GRP):
                    cacc[k, m, sl, :] += jnp.where(c == k, 1.0, 0.0) * dg
        v = jnp.concatenate([jnp.sum(a, axis=0, keepdims=True) for a in ng] + [jnp.zeros((5, BLK), F32)], 0)
        for k in range(3 * GRP):
            nacc[k] += jnp.where(n == k, 1.0, 0.0) * v

    def first(c):
        return c[0], c[1]

    ca, na = first(slot_of(0))
    for r in range(PAIRS):
        stage_a(ca, na, r, r)

    def main(k, carry):
        ca, na = first(slot_of(k))
        tc = jnp.maximum(k - 2, 0)
        cc, _ = first(slot_of(tc))
        finish(jnp.maximum(k - 3, 0), k >= 3)
        for r in range(PAIRS):
            stage_c(cc, r, tc * PAIRS + r)
            stage_b(r)
            stage_a(ca, na, r, k * PAIRS + r)
        return carry

    lax.fori_loop(1, NSLOT, main, 0)
    last = NSLOT - 1
    finish(last - 2, True)
    cc, _ = first(slot_of(last - 1))
    for r in range(PAIRS):
        stage_c(cc, r, (last - 1) * PAIRS + r)
        stage_b(r)
    finish(last - 1, True)
    cc, _ = first(slot_of(last))
    for r in range(PAIRS):
        stage_c(cc, r, last * PAIRS + r)
    finish(last, True)

    crow = jnp.concatenate(
        [jnp.sum(cacc[:, m].reshape(BLK, BLK).T, axis=0, keepdims=True) for m in range(3)]
        + [jnp.zeros((5, BLK), F32)],
        0,
    )
    mine = (lane8 >= QTR * g) & (lane8 < QTR * g + QTR)
    for x in range(GRP):
        moved = pltpu.roll(crow, lax.rem(QTR * g + BLK - QTR * x, BLK), 1)
        res_send[x] = nacc[x]
        res_send[GRP + x] = nacc[GRP + x] - jnp.where(mine, moved, 0.0)
        res_send[2 * GRP + x] = nacc[2 * GRP + x]
    for j, x in enumerate(xs):
        go(rcopy(res_send.at[GRP + x], res_recv.at[own], r_send.at[j], r_recv.at[own], (dm, x)))
    for x in range(GRP):
        go(rcopy(res_send.at[x], res_recv.at[2 * GRP + g], r_send.at[3 + x], r_recv.at[2 * GRP + g], (dn, x)))
        go(rcopy(res_send.at[2 * GRP + x], res_recv.at[g], r_send.at[7 + x], r_recv.at[g], (up, x)))
    out_ref[0] = res_send[own][0:3, :]
    total = jnp.zeros((8, BLK), F32)
    for x in xs:
        rcopy(res_recv.at[GRP + x], res_recv.at[GRP + x], r_send.at[0], r_recv.at[GRP + x], (dm, x)).wait_recv()
        total = total + res_recv[GRP + x]
    for x in range(GRP):
        rcopy(res_recv.at[x], res_recv.at[x], r_send.at[0], r_recv.at[x], (dn, x)).wait_recv()
        total = total + res_recv[x]
        rcopy(
            res_recv.at[2 * GRP + x], res_recv.at[2 * GRP + x], r_send.at[0], r_recv.at[2 * GRP + x], (up, x)
        ).wait_recv()
        total = total + res_recv[2 * GRP + x]
    out_ref[1] = total[0:3, :]
    for c in sends:
        c.wait_send()


def on_device(pos, feat, nw, adj, bw, ew, tc, tn, cnt):
    V = pltpu.VMEM
    vs = pl.BlockSpec(memory_space=pltpu.VMEM)
    sm = pl.BlockSpec(memory_space=pltpu.SMEM)
    D = pltpu.SemaphoreType.DMA
    parts = pl.pallas_call(
        body,
        out_shape=jax.ShapeDtypeStruct((2, 3, BLK), F32),
        in_specs=[vs] * 6 + [sm] * 3,
        out_specs=vs,
        scratch_shapes=[
            V((3 * GRP, BLK, BLK), BF),
            V((3 * GRP, 8, BLK), F32),
            V((GRP, 8, BLK), jnp.int32),
            pltpu.SMEM((GRP, 8, BLK), jnp.int32),
            V((BLK, 256), BF),
            V((GRP, QTR, 256), BF),
            V((3 * GRP, 8, BLK), F32),
            V((3 * GRP, 8, BLK), F32),
            V((3 * GRP, BLK, BLK), F32),
            V((BLK, BLK), F32),
            V((GRP, 3, QTR, BLK), F32),
            V((8 * BLK, BLK), F32),
            V((4 * BLK, BLK), F32),
            V((GRP * PAIRS, 16, BLK), BF),
            V((GRP * PAIRS, 64, BLK), BF),
            V((2 * GRP, BLK, BLK), BF),
            V((8, 16, 2 * BLK), BF),
            V((NSLOT * PAIRS, 16, 2 * BLK), BF),
            V((NSLOT * QTR, 8, BLK), F32),
            V((8 * QTR, BLK), F32),
            V((8 * QTR, BLK), F32),
            V((NSLOT, 5, QTR, BLK), F32),
            V((4 * QTR * NSLOT, BLK), F32),
            V((QTR, BLK), F32),
            V((3 * GRP, 8, BLK), F32),
            V((GRP, 3, QTR, BLK), F32),
            V((PAIRS, BLK, 2 * BLK), BF),
            V((PAIRS, 2 * BLK, 2 * BLK), BF),
            D((3,)),
            D((8,)),
            D((12,)),
            D((3,)),
            D((4,)),
            D((11,)),
            D((12,)),
            D((3,)),
            D((4,)),
            D((11,)),
            D((12,)),
            D,
        ],
        compiler_params=pltpu.CompilerParams(collective_id=0, has_side_effects=True),
        name="allegro_forces",
    )(pos, feat, nw, adj, bw, ew.T, tc, tn, cnt)
    return parts[0] + parts[1]


def solution(mesh):
    placed = (
        P(None, ("dom", "grp")),
        P(None, ("dom", "grp")),
        P(),
        P(None, ("dom", "grp")),
        P(),
        P(),
        P(("dom", "grp")),
        P(("dom", "grp")),
        P(("dom", "grp")),
    )
    return jax.shard_map(
        on_device, mesh=mesh, in_specs=placed, out_specs=P(None, ("dom", "grp")), check_vma=False
    )
```

```python
import jax
import jax.numpy as jnp
from jax import lax
from jax.experimental import pallas as pl
from jax.experimental.pallas import tpu as pltpu
from jax.sharding import PartitionSpec as P

BF = jnp.bfloat16
F32 = jnp.float32
BLK = 128
GRP = 4
SLOTS = 4
NSLOT = GRP * SLOTS
QTR = BLK // GRP
PAIRS = QTR // 2
MESH = pl.DeviceIdType.MESH

RATES = tuple(0.3 * 1.5**b for b in range(8))


def pair_values(h):
    one = jnp.asarray(1.0, BF)
    t = jnp.tanh(h)
    p = one + t
    hid = h * p
    return hid, p + hid * (one - t)


def body(
    pos_h, feat_h, nw_h, adj_h, bw_h, ew_h, tc_h, tn_h, cnt_h, out_ref,
    pos_in, feat_in, nw_in, adj_in, bw_in, ew_in, tc_in, tn_in, cnt_in, in_sem,
    featx, posx, meta, meta_sm, at_send, at_all, res_send, res_recv,
    nf, nwt, ptr, cposb, bt32, bmf, bt, wb, lp, oneh, eye2, rhs, bas, al, pr, ds, y_all, s2_s, nacc, cacc,
    hb, xb,
    fx_send, fz_send, f_recv, a_send, a_recv, p_send, p_recv, m_send, m_recv,
    r_send, r_recv, loc_sem,
):
    g = lax.axis_index("grp")
    dm = lax.axis_index("dom")
    n_dom = lax.axis_size("dom")
    up = lax.rem(dm + 1, n_dom)
    dn = lax.rem(dm + n_dom - 1, n_dom)
    pulls = [
        pltpu.make_async_copy(src, dst, in_sem.at[i])
        for i, (src, dst) in enumerate(
            ((adj_h, adj_in), (nw_h, nw_in), (pos_h, pos_in), (tc_h, tc_in), (tn_h, tn_in), (cnt_h, cnt_in), (feat_h, feat_in), (bw_h, bw_in), (ew_h, ew_in))
        )
    ]
    for c in pulls:
        c.start()
    xs = [lax.rem(g + j, GRP) for j in range(1, GRP)]
    barrier = pltpu.get_barrier_semaphore()
    for x in xs:
        pl.semaphore_signal(barrier, inc=1, device_id=(dm, x), device_id_type=MESH)
    for d in (up, dn):
        for x in range(GRP):
            pl.semaphore_signal(barrier, inc=1, device_id=(d, x), device_id_type=MESH)

    lane8 = lax.broadcasted_iota(jnp.int32, (8, BLK), 1)
    sub8 = lax.broadcasted_iota(jnp.int32, (8, BLK), 0)
    for c in pulls[:6]:
        c.wait()
    mv = jnp.zeros((8, BLK), jnp.int32)
    for t in range(SLOTS):
        mv = jnp.where(lane8 == t, tc_in[t], mv)
        mv = jnp.where(lane8 == SLOTS + t, tn_in[t], mv)
    meta[g] = jnp.where(lane8 == 2 * SLOTS, cnt_in[0], mv)
    posx[GRP + g] = jnp.concatenate([pos_in[...], jnp.zeros((5, BLK), F32)], 0)
    at_send[...] = adj_in[...].astype(F32).T.astype(BF)
    nwt[...] = nw_in[...].astype(F32).T.astype(BF)

    nacc[...] = jnp.zeros_like(nacc)
    cacc[...] = jnp.zeros_like(cacc)
    lane = lax.broadcasted_iota(jnp.int32, (BLK, BLK), 1)
    eye = jnp.where(lane == lax.broadcasted_iota(jnp.int32, (BLK, BLK), 0), 1.0, 0.0).astype(BF)
    eye2[...] = jnp.concatenate([eye, eye], 1)
    row16 = lax.broadcasted_iota(jnp.int32, (16, 2 * BLK), 0)
    side = lax.broadcasted_iota(jnp.int32, (16, 2 * BLK), 1) // BLK
    for r in range(8):
        oneh[r] = jnp.where(row16 == 2 * r + side, 1.0, 0.0).astype(BF)
    for c in pulls[6:]:
        c.wait()
    bwf = bw_in[...].astype(F32)
    own = GRP + g
    featx[own] = feat_in[...]

    def project(b):
        v = jnp.dot(nwt[...], featx[b], preferred_element_type=F32)
        nf[b] = (v.astype(BF).astype(F32) * 0.5).astype(BF)

    project(own)
    pl.semaphore_wait(barrier, 11)

    def rcopy(src, dst, ss, rs, dev):
        return pltpu.make_async_remote_copy(
            src_ref=src, dst_ref=dst, send_sem=ss, recv_sem=rs, device_id=dev, device_id_type=MESH
        )

    sends = []

    def go(c):
        c.start()
        sends.append(c)

    for j, x in enumerate(xs):
        go(rcopy(posx.at[own], posx.at[own], p_send.at[j], p_recv.at[own], (dm, x)))
        go(rcopy(meta.at[g], meta.at[g], m_send.at[j], m_recv.at[g], (dm, x)))
    for x in range(GRP):
        go(rcopy(posx.at[own], posx.at[g], p_send.at[3 + x], p_recv.at[g], (up, x)))
        go(rcopy(posx.at[own], posx.at[2 * GRP + g], p_send.at[7 + x], p_recv.at[2 * GRP + g], (dn, x)))
    for j, x in enumerate(xs):
        rows = pl.ds(pl.multiple_of(QTR * x, QTR), QTR)
        go(rcopy(at_send.at[rows, :], at_all.at[g], a_send.at[j], a_recv.at[g], (dm, x)))
    for j, x in enumerate((xs[0], xs[2], xs[1])):
        go(rcopy(feat_in, featx.at[own], fx_send.at[j], f_recv.at[own], (dm, x)))
    go(rcopy(feat_in, featx.at[g], fz_send.at[0], f_recv.at[g], (up, g)))
    go(rcopy(feat_in, featx.at[2 * GRP + g], fz_send.at[1], f_recv.at[2 * GRP + g], (dn, g)))

    at_all[g] = at_send[pl.ds(pl.multiple_of(QTR * g, QTR), QTR), :]

    for x in xs:
        rcopy(at_all.at[x], at_all.at[x], a_send.at[0], a_recv.at[x], (dm, x)).wait_recv()
    at2 = at_all[...].reshape(BLK, 4 * 64)
    for m in range(4):
        bm = lax.dot_general(
            at2[:, 64 * m : 64 * m + 64], ew_in[...], (((1,), (0,)), ((), ())), preferred_element_type=F32
        )
        hi = bm.astype(BF).astype(F32)
        bt32[pl.ds(m, BLK, stride=8), :] = hi
        bt32[pl.ds(4 + m, BLK, stride=8), :] = bm - hi
        bmf[BLK * m : BLK * m + BLK, :] = bm

    for j, x in enumerate((xs[0], xs[2], xs[1])):
        blk = GRP + x
        rcopy(featx.at[blk], featx.at[blk], fx_send.at[0], f_recv.at[blk], (dm, x)).wait_recv()
        go(rcopy(featx.at[blk], featx.at[x], fz_send.at[2 + 2 * j], f_recv.at[x], (up, g)))
        go(rcopy(featx.at[blk], featx.at[2 * GRP + x], fz_send.at[3 + 2 * j], f_recv.at[2 * GRP + x], (dn, g)))

    wt = (
        jnp.concatenate([bwf, jnp.zeros((BLK - 8, BLK), F32)], 0).T * 0.5
    )
    for c in range(GRP):
        fr = pltpu.roll(featx[GRP + c].astype(F32) * 0.5, lax.rem(16 + BLK - QTR * g, BLK), 1)
        for w in range(2):
            f2 = pltpu.roll(fr, BLK - 16, 1) if w else fr
            lp[2 * c + w] = jnp.where(lane < 8, wt, jnp.where(lane < 16, 0.0, f2)).astype(BF)

    def centre_rows(cp, carry):
        bt[cp] = bt32[pl.ds(pl.multiple_of(16 * cp, 16), 16), :].astype(BF)
        for e in range(2):
            v = [bmf[pl.ds(BLK * m + 2 * cp + e, 8, stride=0), :] * bwf for m in range(4)]
            wb[cp, 32 * e : 32 * e + 32, :] = jnp.concatenate(v, 0).astype(BF)
        return carry

    lax.fori_loop(0, GRP * PAIRS, centre_rows, 0, unroll=8)
    for x in xs:
        rcopy(posx.at[GRP + x], posx.at[GRP + x], p_send.at[0], p_recv.at[GRP + x], (dm, x)).wait_recv()
        rcopy(meta.at[x], meta.at[x], m_send.at[0], m_recv.at[x], (dm, x)).wait_recv()
    for x in range(GRP):
        rcopy(posx.at[x], posx.at[x], p_send.at[0], p_recv.at[x], (dn, x)).wait_recv()
        rcopy(posx.at[2 * GRP + x], posx.at[2 * GRP + x], p_send.at[0], p_recv.at[2 * GRP + x], (up, x)).wait_recv()
    mc = pltpu.make_async_copy(meta, meta_sm, loc_sem)
    mc.start()
    mc.wait()
    pc = jnp.concatenate([posx[GRP + c] for c in range(GRP)] + [jnp.zeros((BLK - 8 * GRP, BLK), F32)], 0)
    ptr[...] = pc.T
    pq = ptr[pl.ds(pl.multiple_of(QTR * g, QTR), QTR), :]
    for c in range(GRP):
        for m in range(3):
            cposb[c, m] = jnp.broadcast_to(pq[:, 8 * c + m : 8 * c + m + 1], (QTR, BLK))

    col = lax.broadcasted_iota(jnp.int32, (8, BLK), 0)
    neg = jnp.zeros((8, BLK), F32)
    for b, rate in enumerate(RATES):
        neg = jnp.where(col == b, -rate, neg)
    half_neg = 0.5 * neg
    z8 = jnp.zeros((8, BLK), F32)

    def slot_of(t):
        gs = t // SLOTS
        ti = lax.rem(t, SLOTS)
        return meta_sm[gs, 0, ti], meta_sm[gs, 0, SLOTS + ti], gs, ti

    def geometry(t, carry):
        c, n, gs, ti = slot_of(t)
        row = posx[n]
        shift = (n // GRP - 1).astype(F32)
        selff = jnp.where(n == c + GRP, 1.0, 0.0)
        npos = [jnp.broadcast_to(row[m : m + 1, :], (8, BLK)) for m in range(3)]
        npos[2] = npos[2] + shift
        for q in range(QTR // 8):
            sl = slice(8 * q, 8 * q + 8)
            d = [npos[m] - cposb[c, m, sl, :] for m in range(3)]
            s2 = d[0] * d[0] + d[1] * d[1] + d[2] * d[2]
            keep = 1.0 - jnp.where(lane8 == sub8 + (QTR * g + 8 * q), selff, 0.0)
            inner = jnp.maximum(1.0 - s2 * 0.25, 0.0)
            env = inner * inner * keep
            s2_s[sl, :] = s2
            hd = [v * 0.5 for v in d]
            ys = [env] + [env * v for v in hd]
            for m in range(4):
                y_all[pl.ds(4 * QTR * t + 32 * q + m, 8, stride=4), :] = ys[m]
            for k, v in enumerate(hd + [env, inner * keep]):
                ds[t, k, sl, :] = v
        for r in range(PAIRS):
            p = t * PAIRS + r
            bs = []
            for e in range(2):
                b = jnp.exp(s2_s[pl.ds(2 * r + e, 8, stride=0), :] * neg)
                bas[2 * p + e] = b * half_neg
                bs.append(b)
            top = jnp.concatenate([jnp.concatenate([bs[0], z8], 0), jnp.concatenate([bs[1], z8], 0)], 1)
            rhs[p] = top.astype(BF)
        return carry

    lax.fori_loop(0, NSLOT, geometry, 0)

    for x in xs:
        project(GRP + x)
    for x in [g, *xs]:
        rcopy(featx.at[x], featx.at[x], fz_send.at[0], f_recv.at[x], (dn, g)).wait_recv()
        project(x)
        rcopy(featx.at[2 * GRP + x], featx.at[2 * GRP + x], fz_send.at[0], f_recv.at[2 * GRP + x], (up, g)).wait_recv()
        project(2 * GRP + x)

    zrow = jnp.zeros((16, 2 * BLK), BF)
    zbt = jnp.zeros((16, BLK), BF)

    def stage_a(b, c, n, r, p):
        w, e = divmod(r, 8)
        right = jnp.concatenate([eye2[...], rhs[p], oneh[e]] + [zrow] * 6, 0)
        left = jnp.concatenate([nf[n], lp[2 * c + w]], 1)
        hb[b, r] = jnp.dot(left, right, preferred_element_type=F32).astype(BF)

    def stage_b(b, r):
        for k in range(0, BLK, 16):
            hid, der = pair_values(hb[b, r, k : k + 16, :])
            xb[b, r, k : k + 16, :] = hid
            xb[b, r, BLK + k : BLK + k + 16, :] = der

    def stage_c(b, c, r, p):
        cp = c * PAIRS + r
        lr = jnp.concatenate(
            [jnp.concatenate([bt[cp], zbt], 1), jnp.concatenate([jnp.zeros((64, BLK), BF), wb[cp]], 1)], 0
        )
        o = jnp.dot(lr, xb[b, r], preferred_element_type=F32)
        for e in range(2):
            i = 2 * r + e
            cut = slice(BLK * e, BLK * e + BLK)
            al[b, 8 * i : 8 * i + 8, :] = o[8 * e : 8 * e + 8, cut]
            first_row = 16 + 32 * e
            v = None
            for m in range(4):
                ym = y_all[pl.ds(4 * (2 * p + e) + m, 8, stride=0), :]
                w = ym * o[first_row + 8 * m : first_row + 8 * m + 8, cut]
                v = w if v is None else v + w
            pr[b, 8 * i : 8 * i + 8, :] = v * bas[2 * p + e]

    def finish(b, t, ready):
        c, n, gs, ti = slot_of(t)
        live = jnp.logical_and(ti < meta_sm[gs, 0, 2 * SLOTS], ready)
        ng = [jnp.zeros((8, BLK), F32)] * 3
        for q in range(QTR // 8):
            sl = slice(8 * q, 8 * q + 8)

            def strip(ref, k):
                return ref[b, pl.ds(64 * q + k, 8, stride=8), :]

            s = strip(pr, 0)
            for j in range(1, 8):
                s = s + strip(pr, j)
            av = [strip(al, m) + strip(al, m + 4) for m in range(4)]
            hd = [ds[t, k, sl, :] for k in range(3)]
            env = ds[t, 3, sl, :]
            ik = ds[t, 4, sl, :]
            eg = av[0] + av[1] * hd[0] + av[2] * hd[1] + av[3] * hd[2]
            sq = (s - 0.5 * eg * ik) * 4.0
            ev = env * 0.5
            for m in range(3):
                dg = jnp.where(live, sq * hd[m] + ev * av[m + 1], 0.0)
                ng[m] = ng[m] + dg
                for k in range(GRP):
                    cacc[k, m, sl, :] += jnp.where(c == k, 1.0, 0.0) * dg
        v = jnp.concatenate([jnp.sum(a, axis=0, keepdims=True) for a in ng] + [jnp.zeros((5, BLK), F32)], 0)
        for k in range(3 * GRP):
            nacc[k] += jnp.where(n == k, 1.0, 0.0) * v

    def first(c):
        return c[0], c[1]

    def step(k, par, do_a, do_b):
        one = 1 - par
        finish(one, jnp.maximum(k - 3, 0), k >= 3)
        tc = jnp.maximum(k - 2, 0)
        cc, _ = first(slot_of(tc))
        if do_a:
            ca, na = first(slot_of(k))
        for r in range(PAIRS):
            stage_c(par, cc, r, tc * PAIRS + r)
            if do_b:
                stage_b(one, r)
            if do_a:
                stage_a(par, ca, na, r, k * PAIRS + r)

    ca, na = first(slot_of(0))
    for r in range(PAIRS):
        stage_a(0, ca, na, r, r)

    def main(j, carry):
        step(2 * j + 1, 1, True, True)
        step(2 * j + 2, 0, True, True)
        return carry

    lax.fori_loop(0, NSLOT // 2 - 1, main, 0)
    step(NSLOT - 1, 1, True, True)
    step(NSLOT, 0, False, True)
    step(NSLOT + 1, 1, False, False)
    finish(1, NSLOT - 1, True)

    crow = jnp.concatenate(
        [jnp.sum(cacc[:, m].reshape(BLK, BLK).T, axis=0, keepdims=True) for m in range(3)]
        + [jnp.zeros((5, BLK), F32)],
        0,
    )
    mine = (lane8 >= QTR * g) & (lane8 < QTR * g + QTR)
    for x in range(GRP):
        moved = pltpu.roll(crow, lax.rem(QTR * g + BLK - QTR * x, BLK), 1)
        res_send[x] = nacc[x]
        res_send[GRP + x] = nacc[GRP + x] - jnp.where(mine, moved, 0.0)
        res_send[2 * GRP + x] = nacc[2 * GRP + x]
    for j, x in enumerate(xs):
        go(rcopy(res_send.at[GRP + x], res_recv.at[own], r_send.at[j], r_recv.at[own], (dm, x)))
    for x in range(GRP):
        go(rcopy(res_send.at[x], res_recv.at[2 * GRP + g], r_send.at[3 + x], r_recv.at[2 * GRP + g], (dn, x)))
        go(rcopy(res_send.at[2 * GRP + x], res_recv.at[g], r_send.at[7 + x], r_recv.at[g], (up, x)))
    out_ref[0] = res_send[own][0:3, :]
    total = jnp.zeros((8, BLK), F32)
    for x in xs:
        rcopy(res_recv.at[GRP + x], res_recv.at[GRP + x], r_send.at[0], r_recv.at[GRP + x], (dm, x)).wait_recv()
        total = total + res_recv[GRP + x]
    for x in range(GRP):
        rcopy(res_recv.at[x], res_recv.at[x], r_send.at[0], r_recv.at[x], (dn, x)).wait_recv()
        total = total + res_recv[x]
        rcopy(
            res_recv.at[2 * GRP + x], res_recv.at[2 * GRP + x], r_send.at[0], r_recv.at[2 * GRP + x], (up, x)
        ).wait_recv()
        total = total + res_recv[2 * GRP + x]
    out_ref[1] = total[0:3, :]
    for c in sends:
        c.wait_send()


def on_device(pos, feat, nw, adj, bw, ew, tc, tn, cnt):
    V = pltpu.VMEM
    vs = pl.BlockSpec(memory_space=pltpu.VMEM)
    hb = pl.BlockSpec(memory_space=pl.ANY)
    D = pltpu.SemaphoreType.DMA
    parts = pl.pallas_call(
        body,
        out_shape=jax.ShapeDtypeStruct((2, 3, BLK), F32),
        in_specs=[hb] * 9,
        out_specs=vs,
        scratch_shapes=[
            V((3, BLK), F32),
            V((BLK, BLK), BF),
            V((BLK, BLK), BF),
            V((2 * BLK, BLK), BF),
            V((8, BLK), BF),
            V((64, BLK), BF),
            pltpu.SMEM((SLOTS,), jnp.int32),
            pltpu.SMEM((SLOTS,), jnp.int32),
            pltpu.SMEM((1,), jnp.int32),
            D((9,)),
            V((3 * GRP, BLK, BLK), BF),
            V((3 * GRP, 8, BLK), F32),
            V((GRP, 8, BLK), jnp.int32),
            pltpu.SMEM((GRP, 8, BLK), jnp.int32),
            V((BLK, 256), BF),
            V((GRP, QTR, 256), BF),
            V((3 * GRP, 8, BLK), F32),
            V((3 * GRP, 8, BLK), F32),
            V((3 * GRP, BLK, BLK), BF),
            V((BLK, BLK), BF),
            V((BLK, BLK), F32),
            V((GRP, 3, QTR, BLK), F32),
            V((8 * BLK, BLK), F32),
            V((4 * BLK, BLK), F32),
            V((GRP * PAIRS, 16, BLK), BF),
            V((GRP * PAIRS, 64, BLK), BF),
            V((2 * GRP, BLK, BLK), BF),
            V((8, 16, 2 * BLK), BF),
            V((BLK, 2 * BLK), BF),
            V((NSLOT * PAIRS, 16, 2 * BLK), BF),
            V((NSLOT * QTR, 8, BLK), F32),
            V((2, 8 * QTR, BLK), F32),
            V((2, 8 * QTR, BLK), F32),
            V((NSLOT, 5, QTR, BLK), F32),
            V((4 * QTR * NSLOT, BLK), F32),
            V((QTR, BLK), F32),
            V((3 * GRP, 8, BLK), F32),
            V((GRP, 3, QTR, BLK), F32),
            V((2, PAIRS, BLK, 2 * BLK), BF),
            V((2, PAIRS, 2 * BLK, 2 * BLK), BF),
            D((3,)),
            D((8,)),
            D((12,)),
            D((3,)),
            D((4,)),
            D((11,)),
            D((12,)),
            D((3,)),
            D((4,)),
            D((11,)),
            D((12,)),
            D,
        ],
        compiler_params=pltpu.CompilerParams(collective_id=0, has_side_effects=True),
        name="allegro_forces",
    )(pos, feat, nw, adj, bw, ew.T, tc, tn, cnt)
    return parts[0] + parts[1]


def solution(mesh):
    placed = (
        P(None, ("dom", "grp")),
        P(None, ("dom", "grp")),
        P(),
        P(None, ("dom", "grp")),
        P(),
        P(),
        P(("dom", "grp")),
        P(("dom", "grp")),
        P(("dom", "grp")),
    )
    return jax.shard_map(
        on_device, mesh=mesh, in_specs=placed, out_specs=P(None, ("dom", "grp")), check_vma=False
    )
```

```python
import jax
import jax.numpy as jnp
from jax import lax
from jax.experimental import pallas as pl
from jax.experimental.pallas import tpu as pltpu
from jax.sharding import PartitionSpec as P

BF = jnp.bfloat16
F32 = jnp.float32
BLK = 128
GRP = 4
SLOTS = 4
NSLOT = GRP * SLOTS
QTR = BLK // GRP
PAIRS = QTR // 2
MESH = pl.DeviceIdType.MESH

RATES = tuple(0.3 * 1.5**b for b in range(8))


def pair_values(h):
    one = jnp.asarray(1.0, BF)
    t = jnp.tanh(h)
    p = one + t
    hid = h * p
    return hid, p + hid * (one - t)


def body(
    pos_h, feat_h, nw_h, adj_h, bw_h, ew_h, tc_h, tn_h, cnt_h, out_ref,
    pos_in, feat_in, nw_in, adj_in, bw_in, ew_in, tc_in, tn_in, cnt_in, in_sem,
    featx, posx, meta, meta_sm, at_send, at_all, res_send, res_recv,
    nf, nwt, ptr, cposb, bt32, bmf, bt, wb, lp, oneh, eye2, rhs, bas, al, pr, ds, y_all, s2_s, nacc, cacc,
    hb, xb,
    fx_send, fz_send, f_recv, a_send, a_recv, p_send, p_recv, m_send, m_recv,
    r_send, r_recv, loc_sem,
):
    g = lax.axis_index("grp")
    dm = lax.axis_index("dom")
    n_dom = lax.axis_size("dom")
    up = lax.rem(dm + 1, n_dom)
    dn = lax.rem(dm + n_dom - 1, n_dom)
    pulls = [
        pltpu.make_async_copy(src, dst, in_sem.at[i])
        for i, (src, dst) in enumerate(
            ((adj_h, adj_in), (nw_h, nw_in), (pos_h, pos_in), (tc_h, tc_in), (tn_h, tn_in), (cnt_h, cnt_in), (feat_h, feat_in), (bw_h, bw_in), (ew_h, ew_in))
        )
    ]
    for c in pulls:
        c.start()
    xs = [lax.rem(g + j, GRP) for j in range(1, GRP)]
    barrier = pltpu.get_barrier_semaphore()
    for x in xs:
        pl.semaphore_signal(barrier, inc=1, device_id=(dm, x), device_id_type=MESH)
    for d in (up, dn):
        for x in range(GRP):
            pl.semaphore_signal(barrier, inc=1, device_id=(d, x), device_id_type=MESH)

    lane8 = lax.broadcasted_iota(jnp.int32, (8, BLK), 1)
    sub8 = lax.broadcasted_iota(jnp.int32, (8, BLK), 0)
    for c in pulls[:6]:
        c.wait()
    mv = jnp.zeros((8, BLK), jnp.int32)
    for t in range(SLOTS):
        mv = jnp.where(lane8 == t, tc_in[t], mv)
        mv = jnp.where(lane8 == SLOTS + t, tn_in[t], mv)
    meta[g] = jnp.where(lane8 == 2 * SLOTS, cnt_in[0], mv)
    posx[GRP + g] = jnp.concatenate([pos_in[...], jnp.zeros((5, BLK), F32)], 0)
    at_send[...] = adj_in[...].astype(F32).T.astype(BF)
    nwt[...] = nw_in[...].astype(F32).T.astype(BF)

    nacc[...] = jnp.zeros_like(nacc)
    cacc[...] = jnp.zeros_like(cacc)
    lane = lax.broadcasted_iota(jnp.int32, (BLK, BLK), 1)
    eye = jnp.where(lane == lax.broadcasted_iota(jnp.int32, (BLK, BLK), 0), 1.0, 0.0).astype(BF)
    eye2[...] = jnp.concatenate([eye, eye], 1)
    row16 = lax.broadcasted_iota(jnp.int32, (16, 2 * BLK), 0)
    side = lax.broadcasted_iota(jnp.int32, (16, 2 * BLK), 1) // BLK
    for r in range(8):
        oneh[r] = jnp.where(row16 == 2 * r + side, 1.0, 0.0).astype(BF)
    for c in pulls[6:]:
        c.wait()
    bwf = bw_in[...].astype(F32)
    own = GRP + g
    featx[own] = feat_in[...]

    def project(*blocks):
        right = jnp.concatenate([featx[b] for b in blocks], 1)
        v = jnp.dot(nwt[...], right, preferred_element_type=F32)
        v = (v.astype(BF).astype(F32) * 0.5).astype(BF)
        for i, b in enumerate(blocks):
            nf[b] = v[:, BLK * i : BLK * i + BLK]

    project(own)
    pl.semaphore_wait(barrier, 11)

    def rcopy(src, dst, ss, rs, dev):
        return pltpu.make_async_remote_copy(
            src_ref=src, dst_ref=dst, send_sem=ss, recv_sem=rs, device_id=dev, device_id_type=MESH
        )

    sends = []

    def go(c):
        c.start()
        sends.append(c)

    for j, x in enumerate(xs):
        go(rcopy(posx.at[own], posx.at[own], p_send.at[j], p_recv.at[own], (dm, x)))
        go(rcopy(meta.at[g], meta.at[g], m_send.at[j], m_recv.at[g], (dm, x)))
    for x in range(GRP):
        go(rcopy(posx.at[own], posx.at[g], p_send.at[3 + x], p_recv.at[g], (up, x)))
        go(rcopy(posx.at[own], posx.at[2 * GRP + g], p_send.at[7 + x], p_recv.at[2 * GRP + g], (dn, x)))
    for j, x in enumerate(xs):
        rows = pl.ds(pl.multiple_of(QTR * x, QTR), QTR)
        go(rcopy(at_send.at[rows, :], at_all.at[g], a_send.at[j], a_recv.at[g], (dm, x)))
    for j, x in enumerate((xs[0], xs[2], xs[1])):
        go(rcopy(feat_in, featx.at[own], fx_send.at[j], f_recv.at[own], (dm, x)))
    go(rcopy(feat_in, featx.at[g], fz_send.at[0], f_recv.at[g], (up, g)))
    go(rcopy(feat_in, featx.at[2 * GRP + g], fz_send.at[1], f_recv.at[2 * GRP + g], (dn, g)))

    at_all[g] = at_send[pl.ds(pl.multiple_of(QTR * g, QTR), QTR), :]

    for x in xs:
        rcopy(at_all.at[x], at_all.at[x], a_send.at[0], a_recv.at[x], (dm, x)).wait_recv()
    at2 = at_all[...].reshape(BLK, 4 * 64)
    for m in range(4):
        bm = lax.dot_general(
            at2[:, 64 * m : 64 * m + 64], ew_in[...], (((1,), (0,)), ((), ())), preferred_element_type=F32
        )
        hi = bm.astype(BF).astype(F32)
        bt32[pl.ds(m, BLK, stride=8), :] = hi
        bt32[pl.ds(4 + m, BLK, stride=8), :] = bm - hi
        bmf[BLK * m : BLK * m + BLK, :] = bm

    for j, x in enumerate((xs[0], xs[2], xs[1])):
        blk = GRP + x
        rcopy(featx.at[blk], featx.at[blk], fx_send.at[0], f_recv.at[blk], (dm, x)).wait_recv()
        go(rcopy(featx.at[blk], featx.at[x], fz_send.at[2 + 2 * j], f_recv.at[x], (up, g)))
        go(rcopy(featx.at[blk], featx.at[2 * GRP + x], fz_send.at[3 + 2 * j], f_recv.at[2 * GRP + x], (dn, g)))

    wt = (
        jnp.concatenate([bwf, jnp.zeros((BLK - 8, BLK), F32)], 0).T * 0.5
    )
    for c in range(GRP):
        fr = pltpu.roll(featx[GRP + c].astype(F32) * 0.5, lax.rem(16 + BLK - QTR * g, BLK), 1)
        for w in range(2):
            f2 = pltpu.roll(fr, BLK - 16, 1) if w else fr
            lp[2 * c + w] = jnp.where(lane < 8, wt, jnp.where(lane < 16, 0.0, f2)).astype(BF)

    def centre_rows(cp, carry):
        bt[cp] = bt32[pl.ds(pl.multiple_of(16 * cp, 16), 16), :].astype(BF)
        for e in range(2):
            v = [bmf[pl.ds(BLK * m + 2 * cp + e, 8, stride=0), :] * bwf for m in range(4)]
            wb[cp, 32 * e : 32 * e + 32, :] = jnp.concatenate(v, 0).astype(BF)
        return carry

    lax.fori_loop(0, GRP * PAIRS, centre_rows, 0, unroll=8)
    for x in xs:
        rcopy(posx.at[GRP + x], posx.at[GRP + x], p_send.at[0], p_recv.at[GRP + x], (dm, x)).wait_recv()
        rcopy(meta.at[x], meta.at[x], m_send.at[0], m_recv.at[x], (dm, x)).wait_recv()
    for x in range(GRP):
        rcopy(posx.at[x], posx.at[x], p_send.at[0], p_recv.at[x], (dn, x)).wait_recv()
        rcopy(posx.at[2 * GRP + x], posx.at[2 * GRP + x], p_send.at[0], p_recv.at[2 * GRP + x], (up, x)).wait_recv()
    mc = pltpu.make_async_copy(meta, meta_sm, loc_sem)
    mc.start()
    mc.wait()
    pc = jnp.concatenate([posx[GRP + c] for c in range(GRP)] + [jnp.zeros((BLK - 8 * GRP, BLK), F32)], 0)
    ptr[...] = pc.T
    pq = ptr[pl.ds(pl.multiple_of(QTR * g, QTR), QTR), :]
    for c in range(GRP):
        for m in range(3):
            cposb[c, m] = jnp.broadcast_to(pq[:, 8 * c + m : 8 * c + m + 1], (QTR, BLK))

    col = lax.broadcasted_iota(jnp.int32, (8, BLK), 0)
    neg = jnp.zeros((8, BLK), F32)
    for b, rate in enumerate(RATES):
        neg = jnp.where(col == b, -rate, neg)
    half_neg = 0.5 * neg
    z8 = jnp.zeros((8, BLK), F32)

    def slot_of(t):
        gs = t // SLOTS
        ti = lax.rem(t, SLOTS)
        return meta_sm[gs, 0, ti], meta_sm[gs, 0, SLOTS + ti], gs, ti

    def geometry(t, carry):
        c, n, gs, ti = slot_of(t)
        row = posx[n]
        shift = (n // GRP - 1).astype(F32)
        selff = jnp.where(n == c + GRP, 1.0, 0.0)
        npos = [jnp.broadcast_to(row[m : m + 1, :], (8, BLK)) for m in range(3)]
        npos[2] = npos[2] + shift
        for q in range(QTR // 8):
            sl = slice(8 * q, 8 * q + 8)
            d = [npos[m] - cposb[c, m, sl, :] for m in range(3)]
            s2 = d[0] * d[0] + d[1] * d[1] + d[2] * d[2]
            keep = 1.0 - jnp.where(lane8 == sub8 + (QTR * g + 8 * q), selff, 0.0)
            inner = jnp.maximum(1.0 - s2 * 0.25, 0.0)
            env = inner * inner * keep
            s2_s[sl, :] = s2
            hd = [v * 0.5 for v in d]
            ys = [env] + [env * v for v in hd]
            for m in range(4):
                y_all[pl.ds(4 * QTR * t + 32 * q + m, 8, stride=4), :] = ys[m]
            for k, v in enumerate(hd + [env, inner * keep]):
                ds[t, k, sl, :] = v
        for r in range(PAIRS):
            p = t * PAIRS + r
            bs = []
            for e in range(2):
                b = jnp.exp(s2_s[pl.ds(2 * r + e, 8, stride=0), :] * neg)
                bas[2 * p + e] = b * half_neg
                bs.append(b)
            top = jnp.concatenate([jnp.concatenate([bs[0], z8], 0), jnp.concatenate([bs[1], z8], 0)], 1)
            rhs[p] = top.astype(BF)
        return carry

    lax.fori_loop(0, NSLOT, geometry, 0)

    project(GRP + xs[0], GRP + xs[1])
    project(GRP + xs[2])
    for x in [g, *xs]:
        rcopy(featx.at[x], featx.at[x], fz_send.at[0], f_recv.at[x], (dn, g)).wait_recv()
        rcopy(featx.at[2 * GRP + x], featx.at[2 * GRP + x], fz_send.at[0], f_recv.at[2 * GRP + x], (up, g)).wait_recv()
        project(x, 2 * GRP + x)

    zrow = jnp.zeros((16, 2 * BLK), BF)
    zbt = jnp.zeros((16, BLK), BF)

    def stage_a(b, c, n, r, p):
        w, e = divmod(r, 8)
        right = jnp.concatenate([eye2[...], rhs[p], oneh[e]] + [zrow] * 6, 0)
        left = jnp.concatenate([nf[n], lp[2 * c + w]], 1)
        hb[b, r] = jnp.dot(left, right, preferred_element_type=F32).astype(BF)

    def stage_b(b, r):
        for k in range(0, BLK, 16):
            hid, der = pair_values(hb[b, r, k : k + 16, :])
            xb[b, r, k : k + 16, :] = hid
            xb[b, r, BLK + k : BLK + k + 16, :] = der

    def stage_c(b, c, r, p):
        cp = c * PAIRS + r
        lr = jnp.concatenate(
            [jnp.concatenate([bt[cp], zbt], 1), jnp.concatenate([jnp.zeros((64, BLK), BF), wb[cp]], 1)], 0
        )
        o = jnp.dot(lr, xb[b, r], preferred_element_type=F32)
        for e in range(2):
            i = 2 * r + e
            cut = slice(BLK * e, BLK * e + BLK)
            al[b, 8 * i : 8 * i + 8, :] = o[8 * e : 8 * e + 8, cut]
            first_row = 16 + 32 * e
            v = None
            for m in range(4):
                ym = y_all[pl.ds(4 * (2 * p + e) + m, 8, stride=0), :]
                w = ym * o[first_row + 8 * m : first_row + 8 * m + 8, cut]
                v = w if v is None else v + w
            pr[b, 8 * i : 8 * i + 8, :] = v * bas[2 * p + e]

    def finish(b, t, ready):
        c, n, gs, ti = slot_of(t)
        live = jnp.logical_and(ti < meta_sm[gs, 0, 2 * SLOTS], ready)
        ng = [jnp.zeros((8, BLK), F32)] * 3
        for q in range(QTR // 8):
            sl = slice(8 * q, 8 * q + 8)

            def strip(ref, k):
                return ref[b, pl.ds(64 * q + k, 8, stride=8), :]

            s = strip(pr, 0)
            for j in range(1, 8):
                s = s + strip(pr, j)
            av = [strip(al, m) + strip(al, m + 4) for m in range(4)]
            hd = [ds[t, k, sl, :] for k in range(3)]
            env = ds[t, 3, sl, :]
            ik = ds[t, 4, sl, :]
            eg = av[0] + av[1] * hd[0] + av[2] * hd[1] + av[3] * hd[2]
            sq = (s - 0.5 * eg * ik) * 4.0
            ev = env * 0.5
            for m in range(3):
                dg = jnp.where(live, sq * hd[m] + ev * av[m + 1], 0.0)
                ng[m] = ng[m] + dg
                for k in range(GRP):
                    cacc[k, m, sl, :] += jnp.where(c == k, 1.0, 0.0) * dg
        v = jnp.concatenate([jnp.sum(a, axis=0, keepdims=True) for a in ng] + [jnp.zeros((5, BLK), F32)], 0)
        for k in range(3 * GRP):
            nacc[k] += jnp.where(n == k, 1.0, 0.0) * v

    def first(c):
        return c[0], c[1]

    def step(k, par, do_a, do_b):
        one = 1 - par
        finish(one, jnp.maximum(k - 3, 0), k >= 3)
        tc = jnp.maximum(k - 2, 0)
        cc, _ = first(slot_of(tc))
        if do_a:
            ca, na = first(slot_of(k))
        for r in range(PAIRS):
            stage_c(par, cc, r, tc * PAIRS + r)
            if do_b:
                stage_b(one, r)
            if do_a:
                stage_a(par, ca, na, r, k * PAIRS + r)

    ca, na = first(slot_of(0))
    for r in range(PAIRS):
        stage_a(0, ca, na, r, r)

    def main(j, carry):
        step(2 * j + 1, 1, True, True)
        step(2 * j + 2, 0, True, True)
        return carry

    lax.fori_loop(0, NSLOT // 2 - 1, main, 0)
    step(NSLOT - 1, 1, True, True)
    step(NSLOT, 0, False, True)
    step(NSLOT + 1, 1, False, False)
    finish(1, NSLOT - 1, True)

    crow = jnp.concatenate(
        [jnp.sum(cacc[:, m].reshape(BLK, BLK).T, axis=0, keepdims=True) for m in range(3)]
        + [jnp.zeros((5, BLK), F32)],
        0,
    )
    mine = (lane8 >= QTR * g) & (lane8 < QTR * g + QTR)
    for x in range(GRP):
        moved = pltpu.roll(crow, lax.rem(QTR * g + BLK - QTR * x, BLK), 1)
        res_send[x] = nacc[x]
        res_send[GRP + x] = nacc[GRP + x] - jnp.where(mine, moved, 0.0)
        res_send[2 * GRP + x] = nacc[2 * GRP + x]
    early = len(sends)
    for j, x in enumerate(xs):
        go(rcopy(res_send.at[GRP + x], res_recv.at[own], r_send.at[j], r_recv.at[own], (dm, x)))
    for x in range(GRP):
        go(rcopy(res_send.at[x], res_recv.at[2 * GRP + g], r_send.at[3 + x], r_recv.at[2 * GRP + g], (dn, x)))
        go(rcopy(res_send.at[2 * GRP + x], res_recv.at[g], r_send.at[7 + x], r_recv.at[g], (up, x)))
    for c in sends[:early]:
        c.wait_send()
    out_ref[0] = res_send[own][0:3, :]
    total = jnp.zeros((8, BLK), F32)
    for x in xs:
        rcopy(res_recv.at[GRP + x], res_recv.at[GRP + x], r_send.at[0], r_recv.at[GRP + x], (dm, x)).wait_recv()
        total = total + res_recv[GRP + x]
    for x in range(GRP):
        rcopy(res_recv.at[x], res_recv.at[x], r_send.at[0], r_recv.at[x], (dn, x)).wait_recv()
        total = total + res_recv[x]
        rcopy(
            res_recv.at[2 * GRP + x], res_recv.at[2 * GRP + x], r_send.at[0], r_recv.at[2 * GRP + x], (up, x)
        ).wait_recv()
        total = total + res_recv[2 * GRP + x]
    out_ref[1] = total[0:3, :]
    for c in sends[early:]:
        c.wait_send()


def on_device(pos, feat, nw, adj, bw, ew, tc, tn, cnt):
    V = pltpu.VMEM
    vs = pl.BlockSpec(memory_space=pltpu.VMEM)
    hb = pl.BlockSpec(memory_space=pl.ANY)
    D = pltpu.SemaphoreType.DMA
    parts = pl.pallas_call(
        body,
        out_shape=jax.ShapeDtypeStruct((2, 3, BLK), F32),
        in_specs=[hb] * 9,
        out_specs=vs,
        scratch_shapes=[
            V((3, BLK), F32),
            V((BLK, BLK), BF),
            V((BLK, BLK), BF),
            V((2 * BLK, BLK), BF),
            V((8, BLK), BF),
            V((64, BLK), BF),
            pltpu.SMEM((SLOTS,), jnp.int32),
            pltpu.SMEM((SLOTS,), jnp.int32),
            pltpu.SMEM((1,), jnp.int32),
            D((9,)),
            V((3 * GRP, BLK, BLK), BF),
            V((3 * GRP, 8, BLK), F32),
            V((GRP, 8, BLK), jnp.int32),
            pltpu.SMEM((GRP, 8, BLK), jnp.int32),
            V((BLK, 256), BF),
            V((GRP, QTR, 256), BF),
            V((3 * GRP, 8, BLK), F32),
            V((3 * GRP, 8, BLK), F32),
            V((3 * GRP, BLK, BLK), BF),
            V((BLK, BLK), BF),
            V((BLK, BLK), F32),
            V((GRP, 3, QTR, BLK), F32),
            V((8 * BLK, BLK), F32),
            V((4 * BLK, BLK), F32),
            V((GRP * PAIRS, 16, BLK), BF),
            V((GRP * PAIRS, 64, BLK), BF),
            V((2 * GRP, BLK, BLK), BF),
            V((8, 16, 2 * BLK), BF),
            V((BLK, 2 * BLK), BF),
            V((NSLOT * PAIRS, 16, 2 * BLK), BF),
            V((NSLOT * QTR, 8, BLK), F32),
            V((2, 8 * QTR, BLK), F32),
            V((2, 8 * QTR, BLK), F32),
            V((NSLOT, 5, QTR, BLK), F32),
            V((4 * QTR * NSLOT, BLK), F32),
            V((QTR, BLK), F32),
            V((3 * GRP, 8, BLK), F32),
            V((GRP, 3, QTR, BLK), F32),
            V((2, PAIRS, BLK, 2 * BLK), BF),
            V((2, PAIRS, 2 * BLK, 2 * BLK), BF),
            D((3,)),
            D((8,)),
            D((12,)),
            D((3,)),
            D((4,)),
            D((11,)),
            D((12,)),
            D((3,)),
            D((4,)),
            D((11,)),
            D((12,)),
            D,
        ],
        compiler_params=pltpu.CompilerParams(collective_id=0, has_side_effects=True),
        name="allegro_forces",
    )(pos, feat, nw, adj, bw, ew.T, tc, tn, cnt)
    return parts[0] + parts[1]


def solution(mesh):
    placed = (
        P(None, ("dom", "grp")),
        P(None, ("dom", "grp")),
        P(),
        P(None, ("dom", "grp")),
        P(),
        P(),
        P(("dom", "grp")),
        P(("dom", "grp")),
        P(("dom", "grp")),
    )
    return jax.shard_map(
        on_device, mesh=mesh, in_specs=placed, out_specs=P(None, ("dom", "grp")), check_vma=False
    )
```
